512 devices in a mesh: wide: 32 (over z_lo, x, core), narrow: 16 (over z_hi, y).
Axes of the slice: x: 4, y: 8, z: 8 (z_hi: 2, z_lo: 4; z = z_hi * 4 + z_lo), core: 2. Of those that a mesh axis runs over, the one named last changes fastest.
Arguments:
- exposures: bfloat16 [4, 512, 12288], P(None, 'narrow', 'wide'), may hold values from -6 to 6
- basis_kernels: bfloat16 [5, 21, 21], replicated, may hold values from -0.25 to 0.25
- poly_coef: float32 [4, 5, 6], replicated, may hold values from -3 to 3
- exposure_weight: float32 [4], replicated, may hold values from 0.5 to 2
- row_start: int32 [4], replicated, may hold values from 0 to 256, as said below
- row_count: int32 [4], replicated, may hold values from 128 to 512, as said below
- filter_taps: float32 [21], replicated, may hold values from -1.5 to 1.5
Outputs:
- coadded: float32 [512, 12288], P('narrow', 'wide')
- detection: float32 [512, 12288], P('narrow', 'wide')
The draws below stay inside these ranges and needn't reach their ends.
Inputs may be any that keep to these rules, and one draw needn't show every extreme that they name: Each row_start is a multiple of 32; row_start[0] is 0 and row_start + row_count never exceeds 512. Each row_count is a multiple of 8; exposure 0 covers the whole band.
All inputs are finite; a program needn't handle non-finite values.
Results may differ from the reference program's by a relative error of at most 0.0003.
Values may be sent and summed in bfloat16 or wider, within the bound.
A program may use at most 64 MiB of HBM per device.

```python
import math
import jax
import jax.numpy as jnp
from jax import lax

EXPOSURES = 4
KERNELS = 5
KSIZE = 21
TH = 32
NR = 512
NC = 12288


def coverage_table(key):
    folded = jax.random.fold_in(key, 31)
    key_start, key_count = jax.random.split(folded)
    blocks = NR // TH
    starts = TH * jax.random.randint(key_start, (EXPOSURES,), 0, blocks // 2 + 1)
    starts = starts.at[0].set(0)
    starts = starts.at[1].set(TH * (blocks // 2))
    spare_room = (NR - starts - NR // 4) // 8 + 1
    drawn_values = jax.random.randint(key_count, (EXPOSURES,), 0, 1 << 20)
    counts = NR // 4 + 8 * (drawn_values % spare_room)
    counts = counts.at[0].set(NR)
    counts = counts.at[1].set(NR // 4)
    return (starts.astype(jnp.int32), counts.astype(jnp.int32))


def draw_row_start(key, part):
    return coverage_table(key)[0]


def draw_row_count(key, part):
    return coverage_table(key)[1]


def levels(rng, shape, shards, smallest, largest):
    factor_of, own = 1.0, jax.random.fold_in(rng, 6)
    for dim, parts in shards:
        heights = jnp.exp(jax.random.uniform(jax.random.fold_in(own, dim), (parts,), jnp.float32, smallest / len(shards), largest / len(shards)))
        factor_of = factor_of * jnp.repeat(heights, shape[dim] // parts).reshape([-1 if axis == dim else 1 for axis in range(len(shape))])
    return factor_of


def scatter_about(own_key, shape, spread, limit, shards=(), kind=jnp.bfloat16):
    array = jax.random.normal(own_key, shape, jnp.float32) * spread
    if len(shards) > 0:
        array = levels(own_key, shape, shards, -0.22, 0.18) * array
    return jnp.clip(array, min=-limit, max=limit).astype(kind)


def setup_inputs(seed: int = 0) -> dict:
    splits = jax.random.split(jax.random.key(seed), 8)
    exposures = scatter_about(splits[0], (EXPOSURES, NR, NC), 1.0, 6.0, ((1, 16), (2, 32)))
    basis_kernels = scatter_about(splits[1], (KERNELS, KSIZE, KSIZE), (KSIZE * KSIZE) ** -0.5, 0.25)
    poly_coef = scatter_about(splits[2], (EXPOSURES, KERNELS, 6), 0.5, 3.0, (), jnp.float32)
    exposure_weight = jnp.clip(jnp.exp(jax.random.uniform(splits[3], (EXPOSURES,), jnp.float32, math.log(0.5), math.log(2.0))), 0.5, 2.0)
    row_start = draw_row_start(jax.random.fold_in(splits[7], 71), 0)
    row_count = draw_row_count(jax.random.fold_in(splits[7], 71), 0)
    filter_taps = scatter_about(splits[6], (KSIZE,), 0.25, 1.5, (), jnp.float32)
    return dict(exposures=exposures, basis_kernels=basis_kernels, poly_coef=poly_coef, exposure_weight=exposure_weight, row_start=row_start, row_count=row_count, filter_taps=filter_taps)


def respond(image, basis_kernels):
    padded = jnp.pad(image, 10)[None, None]
    return lax.conv_general_dilated(padded, basis_kernels[:, None], (1, 1), "VALID", dimension_numbers=("NCHW", "OIHW", "NCHW"), preferred_element_type=jnp.float32)[0]


def reference(exposures, basis_kernels, poly_coef, exposure_weight, row_start, row_count, filter_taps):
    row_index = jnp.arange(NR, dtype=jnp.int32)
    col_index = jnp.arange(NC, dtype=jnp.int32)
    y_coord = ((2 * row_index + 1).astype(jnp.float32) / NR - 1.0)[:, None]
    x_coord = ((2 * col_index + 1).astype(jnp.float32) / NC - 1.0)[None, :]
    numerator = jnp.zeros((NR, NC), jnp.float32)
    denominator = jnp.zeros((NR, 1), jnp.float32)
    for member in range(EXPOSURES):
        framed = jnp.concatenate([jnp.zeros((NR, NC), exposures.dtype), exposures[member]], 0)
        placed = lax.dynamic_slice_in_dim(framed, (NR - row_start[member]).astype(jnp.int32), NR, 0)
        inside = (row_index >= row_start[member]) & (row_index < row_start[member] + row_count[member])
        placed = jnp.where(inside[:, None], placed, jnp.zeros((), exposures.dtype))
        response = respond(placed, basis_kernels)
        matched = jnp.zeros((NR, NC), jnp.float32)
        for kernel in range(KERNELS):
            coeffs = poly_coef[member, kernel]
            spatial = coeffs[0] + coeffs[1] * x_coord + coeffs[2] * y_coord + coeffs[3] * x_coord * x_coord + coeffs[4] * x_coord * y_coord + coeffs[5] * y_coord * y_coord
            matched = matched + spatial * response[kernel]
        weighting = exposure_weight[member] * inside.astype(jnp.float32)[:, None]
        numerator = numerator + weighting * matched
        denominator = denominator + weighting
    coadded = numerator / denominator
    padded = jnp.pad(coadded, ((0, 0), (10, 10)))
    across = filter_taps[0] * padded[:, 0:NC]
    for offset in range(1, KSIZE):
        across = across + filter_taps[offset] * padded[:, offset:offset + NC]
    padded = jnp.pad(across, ((10, 10), (0, 0)))
    detection = filter_taps[0] * padded[0:NR]
    for offset in range(1, KSIZE):
        detection = detection + filter_taps[offset] * padded[offset:offset + NR]
    return coadded, detection
```

```python
import functools

import jax
import jax.numpy as jnp
from jax import lax
from jax.experimental import pallas as pl
from jax.experimental.pallas import tpu as pltpu
from jax.sharding import PartitionSpec as P

LANES = 128
SUBLANES = 8


def moved(array, shift):
    peers = lax.axis_size("narrow")
    if shift == 0:
        return array
    return lax.ppermute(array, "narrow", [(i, i + shift) for i in range(peers - shift)])


def placed_tiles(tiles, shifts, radix):
    for scale, digits in (
        (radix, [shift // radix for shift in shifts]),
        (1, [shift % radix for shift in shifts]),
    ):
        choice = digits[0]
        for digit in digits[1:]:
            choice = choice * radix + digit

        def branch(index, scale=scale):
            own = []
            for _ in tiles:
                own.append(index % radix)
                index //= radix
            own = own[::-1]

            def run(*operands):
                return tuple(moved(op, scale * step) for op, step in zip(operands, own))

            return run

        tiles = lax.switch(choice, [branch(i) for i in range(radix ** len(tiles))], *tiles)
    return tiles


def padded(array, axis, dim, width):
    peers, length = lax.axis_size(axis), array.shape[dim]
    up = [(i, i + 1) for i in range(peers - 1)]
    down = [(j, i) for i, j in up]
    before = lax.ppermute(lax.slice_in_dim(array, length - width, length, axis=dim), axis, up)
    after = lax.ppermute(lax.slice_in_dim(array, 0, width, axis=dim), axis, down)
    return jnp.concatenate([before, array, after], axis=dim)


def coadd_kernel(
    sizes,
    poly_ref,
    weight_ref,
    start_ref,
    count_ref,
    taps_ref,
    window_ref,
    seed_ref,
    coadd_ref,
    detect_ref,
    table,
    shifted,
    lhs,
    sums,
    spread,
):
    members, kernels, side, band_rows, band_cols, tile_rows, tile_cols = sizes
    half = side // 2
    step = LANES - (side - 1)
    blocks = pl.cdiv(tile_cols + 2 * half, step)
    rows = pl.cdiv(tile_rows + 2 * half, SUBLANES) * SUBLANES
    row_base = lax.axis_index("narrow") * tile_rows
    col_base = lax.axis_index("wide") * tile_cols

    for a in range(side):
        for k in range(kernels):
            seed = jnp.broadcast_to(seed_ref[k * side + a : k * side + a + 1, :], (LANES, LANES))
            band = pltpu.roll(seed, 0, 1, stride=1, stride_axis=0)
            table[a * LANES : (a + 1) * LANES, k * LANES : (k + 1) * LANES] = band.astype(
                jnp.bfloat16
            )

    all_rows = shifted.shape[1]
    window_rows = (
        row_base - 2 * half + lax.broadcasted_iota(jnp.int32, (all_rows, LANES), 0)
    )
    lane_in = lax.broadcasted_iota(jnp.int32, (all_rows, LANES), 1)
    out_row = row_base - half + lax.broadcasted_iota(jnp.int32, (rows, LANES), 0)
    y = (2 * out_row + 1).astype(jnp.float32) / band_rows - 1.0
    lane = lax.broadcasted_iota(jnp.int32, (rows, LANES), 1)
    cols = [col_base - half + block * step + lane for block in range(blocks)]
    denominator = jnp.zeros((rows, LANES), jnp.float32)
    sums[...] = jnp.zeros_like(sums)

    for e in range(members):
        first, total = start_ref[e], count_ref[e]
        inside = (out_row >= first) & (out_row < first + total)
        weighting = weight_ref[e] * inside.astype(jnp.float32)
        denominator = denominator + weighting
        touches = (first < row_base + tile_rows + half) & (first + total > row_base - half)

        @pl.when(touches)
        def _(e=e, first=first, total=total, weighting=weighting):
            valid = (window_rows >= first) & (window_rows < first + total)
            parts = []
            for tile in range(window_ref.shape[2] // LANES):
                part = window_ref[e, :, tile * LANES : (tile + 1) * LANES].astype(jnp.float32)
                parts.append(jnp.where(valid, part, 0.0))
            for block in range(blocks):
                tile, offset = divmod(block * step, LANES)
                here = parts[tile]
                if offset:
                    here = pltpu.roll(here, LANES - offset, 1)
                    if tile + 1 < len(parts):
                        after = pltpu.roll(parts[tile + 1], LANES - offset, 1)
                    else:
                        after = jnp.zeros_like(here)
                    here = jnp.where(lane_in < LANES - offset, here, after)
                shifted[block] = here
            for a in range(side):
                piece = jnp.concatenate(
                    [shifted[block, a : a + rows, :] for block in range(blocks)], axis=0
                )
                lhs[:, a * LANES : (a + 1) * LANES] = piece.astype(jnp.bfloat16)
            response = jnp.dot(lhs[...], table[...], preferred_element_type=jnp.float32)
            for block in range(blocks):
                x = (2 * cols[block] + 1).astype(jnp.float32) / band_cols - 1.0
                matched = jnp.zeros((rows, LANES), jnp.float32)
                for k in range(kernels):
                    p = [poly_ref[(e * kernels + k) * 6 + i] for i in range(6)]
                    spatial = (p[0] + y * (p[2] + p[5] * y)) + x * ((p[1] + p[4] * y) + p[3] * x)
                    matched = matched + spatial * response[
                        block * rows : (block + 1) * rows, k * LANES : (k + 1) * LANES
                    ]
                sums[block] += weighting * matched

    in_rows = (out_row >= 0) & (out_row < band_rows)
    divisor = jnp.where(in_rows, denominator, 1.0)
    coadds = []
    for block in range(blocks):
        keep = in_rows & (cols[block] >= 0) & (cols[block] < band_cols)
        coadds.append(jnp.where(keep, sums[block] / divisor, 0.0))
    tiles = spread.shape[1] // LANES
    for tile in range(tiles):
        line = jnp.zeros((rows, LANES), jnp.float32)
        for block in range(blocks):
            low = block * step - tile * LANES
            if low + step <= 0 or low >= LANES:
                continue
            turned = pltpu.roll(coadds[block], low % LANES, 1) if low % LANES else coadds[block]
            line = jnp.where((lane >= low) & (lane < low + step), turned, line)
        spread[:, tile * LANES : (tile + 1) * LANES] = line

    def ahead(parts, tile, offset):
        if offset == 0:
            return parts[tile]
        lanes = lax.broadcasted_iota(jnp.int32, parts[tile].shape, 1)
        here = pltpu.roll(parts[tile], LANES - offset, 1)
        after = pltpu.roll(parts[tile + 1], LANES - offset, 1)
        return jnp.where(lanes < LANES - offset, here, after)

    out_tiles = tile_cols // LANES
    own = [
        spread[half : half + tile_rows, i * LANES : (i + 1) * LANES] for i in range(tiles)
    ]
    for i in range(out_tiles):
        coadd_ref[:, i * LANES : (i + 1) * LANES] = ahead(own, i, half)
    down = []
    for i in range(tiles):
        total = taps_ref[0] * spread[0:tile_rows, i * LANES : (i + 1) * LANES]
        for t in range(1, side):
            total = total + taps_ref[t] * spread[
                t : t + tile_rows, i * LANES : (i + 1) * LANES
            ]
        down.append(total)
    for i in range(out_tiles):
        total = taps_ref[0] * ahead(down, i, 0)
        for t in range(1, side):
            total = total + taps_ref[t] * ahead(down, i, t)
        detect_ref[:, i * LANES : (i + 1) * LANES] = total


def on_device(
    exposures, basis_kernels, poly_coef, exposure_weight, row_start, row_count, filter_taps
):
    members, tile_rows, tile_cols = exposures.shape
    kernels, side = basis_kernels.shape[:2]
    half = side // 2
    band_rows = tile_rows * lax.axis_size("narrow")
    band_cols = tile_cols * lax.axis_size("wide")
    step = LANES - (side - 1)
    blocks = pl.cdiv(tile_cols + 2 * half, step)
    rows = pl.cdiv(tile_rows + 2 * half, SUBLANES) * SUBLANES
    all_rows = pl.cdiv(rows + side - 1, 2 * SUBLANES) * 2 * SUBLANES

    shifts = [row_start[e] // tile_rows for e in range(1, members)]
    tiles = placed_tiles(tuple(exposures[e] for e in range(1, members)), shifts, 3)
    window = jnp.stack([exposures[0], *tiles])
    window = padded(window, "narrow", 1, 2 * half)
    window = padded(window, "wide", 2, 2 * half)
    width = pl.cdiv(tile_cols + 4 * half, LANES) * LANES
    window = jnp.pad(
        window, ((0, 0), (0, all_rows - window.shape[1]), (0, width - window.shape[2]))
    )
    taps = basis_kernels.astype(jnp.float32).reshape(kernels * side, side)
    seed = jnp.concatenate(
        [taps[:, :1], jnp.zeros((kernels * side, step - 1), jnp.float32), taps[:, :0:-1]], axis=1
    )
    sizes = (members, kernels, side, band_rows, band_cols, tile_rows, tile_cols)
    out = jax.ShapeDtypeStruct((tile_rows, tile_cols), jnp.float32)
    scalars = pl.BlockSpec(memory_space=pltpu.SMEM)
    return pl.pallas_call(
        functools.partial(coadd_kernel, sizes),
        out_shape=(out, out),
        in_specs=[scalars] * 5 + [pl.BlockSpec(memory_space=pltpu.VMEM)] * 2,
        out_specs=(pl.BlockSpec(memory_space=pltpu.VMEM),) * 2,
        scratch_shapes=[
            pltpu.VMEM((side * LANES, kernels * LANES), jnp.bfloat16),
            pltpu.VMEM((blocks, all_rows, LANES), jnp.float32),
            pltpu.VMEM((blocks * rows, side * LANES), jnp.bfloat16),
            pltpu.VMEM((blocks, rows, LANES), jnp.float32),
            pltpu.VMEM((rows, width), jnp.float32),
        ],
        name="coadd",
    )(
        poly_coef.reshape(-1),
        exposure_weight,
        row_start,
        row_count,
        filter_taps,
        window,
        seed,
    )


def solution(mesh):
    placed = (P(None, "narrow", "wide"), P(), P(), P(), P(), P(), P())
    return jax.shard_map(
        on_device,
        mesh=mesh,
        in_specs=placed,
        out_specs=(P("narrow", "wide"), P("narrow", "wide")),
        check_vma=False,
    )
```

```python
import functools

import jax
import jax.numpy as jnp
from jax import lax
from jax.experimental import pallas as pl
from jax.experimental.pallas import tpu as pltpu
from jax.sharding import PartitionSpec as P

LANES = 128
SUBLANES = 8


MESH = pl.DeviceIdType.MESH


def exchange_kernel(
    shift_ref, x_ref, window, left, right, far, near, across, cross, held, sent, got, column_sem
):
    members, tile_rows = x_ref.shape[:2]
    ring = lax.axis_size("narrow") // 2
    me = lax.axis_index("narrow")
    column, columns = lax.axis_index("wide"), lax.axis_size("wide")
    second, place = me // ring, me % ring

    def on_ring(turn):
        return {"narrow": second * ring + (place + turn + ring) % ring}

    last_first = (second == 0) & (place == ring - 1)
    first_second = (second == 1) & (place == 0)
    last_second = (second == 1) & (place == ring - 1)
    other = {"narrow": (1 - second) * ring + place}
    over_end = {"narrow": (1 - second) * ring + (ring - 1 - place)}

    barrier = pltpu.get_barrier_semaphore()
    for peer in (on_ring(1), on_ring(-1), on_ring(3), on_ring(-3), other):
        pl.semaphore_signal(barrier, inc=1, device_id=peer, device_id_type=MESH)

    @pl.when(last_first | first_second)
    def _():
        pl.semaphore_signal(barrier, inc=1, device_id=over_end, device_id_type=MESH)

    @pl.when(column > 0)
    def _():
        pl.semaphore_signal(barrier, inc=1, device_id={"wide": column - 1}, device_id_type=MESH)

    @pl.when(column < columns - 1)
    def _():
        pl.semaphore_signal(barrier, inc=1, device_id={"wide": column + 1}, device_id_type=MESH)

    count = 5 + (last_first | first_second).astype(jnp.int32)
    count = count + (column > 0).astype(jnp.int32) + (column < columns - 1).astype(jnp.int32)
    pl.semaphore_wait(barrier, count)

    def copy(src, dst, slot, peer):
        return pltpu.make_async_remote_copy(
            src_ref=src,
            dst_ref=dst,
            send_sem=sent.at[slot],
            recv_sem=got.at[slot],
            device_id=peer,
            device_id_type=MESH,
        )

    def own(e):
        return window.at[e, tile_rows : 2 * tile_rows, :]

    def turns(src, into, slot, e, by):
        return [
            copy(src, into.at[e, i], slot + 2 * e + i, on_ring(turn))
            for i, turn in enumerate((by, -by))
        ]

    def pick(e, digit, stay, moved):
        value = jnp.full(stay.shape, shift_ref[2 * e + digit], jnp.int32)
        up, down = moved[e, 0].astype(jnp.float32), moved[e, 1].astype(jnp.float32)
        chosen = jnp.where(value == 1, up, jnp.where(value == -1, down, stay.astype(jnp.float32)))
        return chosen.astype(jnp.bfloat16)

    window[0, tile_rows : 2 * tile_rows, :] = x_ref[0]

    def rows_out(e):
        above = copy(own(e), window.at[e, 0:tile_rows, :], 16 + 2 * e, on_ring(1))
        below = copy(
            own(e), window.at[e, 2 * tile_rows : 3 * tile_rows, :], 17 + 2 * e, on_ring(-1)
        )
        return above, below

    def wrapped(e):
        return copy(across.at[e], window.at[e, 0:tile_rows, :], 16 + 2 * e, on_ring(1))

    def over(e):
        return copy(window.at[e, tile_rows : 2 * tile_rows, :], across.at[e], 24 + e, other)

    def end(e):
        return copy(x_ref.at[e], cross.at[e], 28 + e, over_end)

    first = [turns(x_ref.at[e], far, 0, e, 3) for e in range(1, members)]
    for pair in first:
        for c in pair:
            c.start()

    @pl.when(first_second)
    def _():
        for e in range(members):
            end(e).start()

    @pl.when(last_first)
    def _():
        over(0).start()

    second_turns = []
    for e in range(1, members):
        for c in first[e - 1]:
            c.wait_recv()
        held[e] = pick(e, 0, x_ref[e], far)
        pair = turns(held.at[e], near, 8, e, 1)
        for c in pair:
            c.start()
        second_turns.append(pair)
    for e in range(1, members):
        for c in second_turns[e - 1]:
            c.wait_recv()
        window[e, tile_rows : 2 * tile_rows, :] = pick(e, 1, held[e], near)

        @pl.when(second == 0)
        def _(e=e):
            over(e).start()

    @pl.when(last_second)
    def _():
        over(0).wait_recv()
        wrapped(0).start()

    @pl.when(jnp.logical_not(last_second))
    def _():
        rows_out(0)[0].start()

    rows_out(0)[1].start()
    for e in range(1, members):

        @pl.when(second == 1)
        def _(e=e):
            over(e).wait_recv()
            here = window[e, tile_rows : 2 * tile_rows, :].astype(jnp.float32)
            passed = jnp.full(here.shape, shift_ref[2 * members + e] - place, jnp.int32)
            chosen = jnp.where(passed > 0, across[e].astype(jnp.float32), here)
            window[e, tile_rows : 2 * tile_rows, :] = chosen.astype(jnp.bfloat16)

        @pl.when(last_second)
        def _(e=e):
            wrapped(e).start()

        @pl.when(jnp.logical_not(last_second))
        def _(e=e):
            rows_out(e)[0].start()

        rows_out(e)[1].start()

    for e in range(members):
        for c in rows_out(e):
            c.wait_recv()

    @pl.when(last_first)
    def _():
        for e in range(members):
            end(e).wait_recv()
            here = window[e, 2 * tile_rows : 3 * tile_rows, :].astype(jnp.float32)
            still = jnp.full(here.shape, shift_ref[2 * members + e], jnp.int32)
            chosen = jnp.where(still == 0, cross[e].astype(jnp.float32), here)
            window[e, 2 * tile_rows : 3 * tile_rows, :] = chosen.astype(jnp.bfloat16)

    width = window.shape[2]

    def sideways(lanes, into, slot, peer):
        return pltpu.make_async_remote_copy(
            src_ref=window.at[:, :, lanes : lanes + LANES],
            dst_ref=into,
            send_sem=column_sem.at[slot],
            recv_sem=column_sem.at[2 + slot],
            device_id={"wide": peer},
            device_id_type=MESH,
        )

    to_left = sideways(0, right, 0, column - 1)
    to_right = sideways(width - LANES, left, 1, column + 1)

    @pl.when(column > 0)
    def _():
        to_left.start()

    @pl.when(column < columns - 1)
    def _():
        to_right.start()

    for e in range(1, members):
        for c in first[e - 1] + second_turns[e - 1]:
            c.wait_send()
    for e in range(members):
        for c in rows_out(e):
            c.wait_send()

    @pl.when(second == 0)
    def _():
        for e in range(1, members):
            over(e).wait_send()

    @pl.when(last_first)
    def _():
        over(0).wait_send()

    @pl.when(first_second)
    def _():
        for e in range(members):
            end(e).wait_send()

    @pl.when(column > 0)
    def _():
        to_left.wait_send()
        to_right.wait_recv()

    @pl.when(column < columns - 1)
    def _():
        to_right.wait_send()
        to_left.wait_recv()


def exchange(exposures, row_start):
    members, tile_rows, tile_cols = exposures.shape
    ring = lax.axis_size("narrow") // 2
    moves = row_start // tile_rows
    turn = (moves + ring // 2 - 1) % ring - (ring // 2 - 1)
    high = (turn >= 2).astype(jnp.int32) - (turn <= -2).astype(jnp.int32)
    digits = jnp.stack([high, turn - 3 * high], axis=1).reshape(-1)
    dtype = exposures.dtype
    vmem = pl.BlockSpec(memory_space=pltpu.VMEM)
    edge = jax.ShapeDtypeStruct((members, 3 * tile_rows, LANES), dtype)
    tile = (members, tile_rows, tile_cols)
    return pl.pallas_call(
        exchange_kernel,
        out_shape=(jax.ShapeDtypeStruct((members, 3 * tile_rows, tile_cols), dtype), edge, edge),
        in_specs=[pl.BlockSpec(memory_space=pltpu.SMEM), vmem],
        out_specs=(vmem,) * 3,
        scratch_shapes=[
            pltpu.VMEM((members, 2, tile_rows, tile_cols), dtype),
            pltpu.VMEM((members, 2, tile_rows, tile_cols), dtype),
            pltpu.VMEM(tile, dtype),
            pltpu.VMEM(tile, dtype),
            pltpu.VMEM(tile, dtype),
            pltpu.SemaphoreType.DMA((32,)),
            pltpu.SemaphoreType.DMA((32,)),
            pltpu.SemaphoreType.DMA((4,)),
        ],
        compiler_params=pltpu.CompilerParams(collective_id=0, has_side_effects=True),
        name="exchange",
    )(jnp.concatenate([digits, moves]), exposures)


def coadd_kernel(
    sizes,
    poly_ref,
    weight_ref,
    start_ref,
    count_ref,
    taps_ref,
    window_ref,
    left_ref,
    right_ref,
    seed_ref,
    coadd_ref,
    detect_ref,
    table,
    shifted,
    lhs,
    sums,
    spread,
):
    members, kernels, side, band_rows, band_cols, tile_rows, tile_cols = sizes
    half = side // 2
    step = LANES - (side - 1)
    blocks = pl.cdiv(tile_cols + 2 * half, step)
    rows = pl.cdiv(tile_rows + 2 * half, SUBLANES) * SUBLANES
    row_base = lax.axis_index("narrow") * tile_rows
    col_base = lax.axis_index("wide") * tile_cols

    for a in range(side):
        for k in range(kernels):
            seed = jnp.broadcast_to(seed_ref[k * side + a : k * side + a + 1, :], (LANES, LANES))
            band = pltpu.roll(seed, 0, 1, stride=1, stride_axis=0)
            table[a * LANES : (a + 1) * LANES, k * LANES : (k + 1) * LANES] = band.astype(
                jnp.bfloat16
            )

    all_rows, lead = shifted.shape[1], tile_rows - 2 * half
    window_rows = (
        row_base - tile_rows + lax.broadcasted_iota(jnp.int32, (all_rows, LANES), 0)
    )
    lane_in = lax.broadcasted_iota(jnp.int32, (all_rows, LANES), 1)
    out_row = row_base - half + lax.broadcasted_iota(jnp.int32, (rows, LANES), 0)
    y = (2 * out_row + 1).astype(jnp.float32) / band_rows - 1.0
    lane = lax.broadcasted_iota(jnp.int32, (rows, LANES), 1)
    cols = [col_base - half + block * step + lane for block in range(blocks)]
    denominator = jnp.zeros((rows, LANES), jnp.float32)
    sums[...] = jnp.zeros_like(sums)

    for e in range(members):
        first, total = start_ref[e], count_ref[e]
        inside = (out_row >= first) & (out_row < first + total)
        weighting = weight_ref[e] * inside.astype(jnp.float32)
        denominator = denominator + weighting
        touches = (first < row_base + tile_rows + half) & (first + total > row_base - half)

        @pl.when(touches)
        def _(e=e, first=first, total=total, weighting=weighting):
            valid = (window_rows >= first) & (window_rows < first + total)
            parts = []
            pieces = [left_ref[e]]
            for tile in range(window_ref.shape[2] // LANES):
                pieces.append(window_ref[e, :, tile * LANES : (tile + 1) * LANES])
            pieces.append(right_ref[e])
            for tile, piece in enumerate(pieces):
                col = lane_in + (col_base + (tile - 1) * LANES)
                keep = valid & (col >= 0) & (col < band_cols)
                parts.append(jnp.where(keep, piece.astype(jnp.float32), 0.0))
            for block in range(blocks):
                tile, offset = divmod(LANES - 2 * half + block * step, LANES)
                here = parts[tile]
                if offset:
                    here = pltpu.roll(here, LANES - offset, 1)
                    if tile + 1 < len(parts):
                        after = pltpu.roll(parts[tile + 1], LANES - offset, 1)
                    else:
                        after = jnp.zeros_like(here)
                    here = jnp.where(lane_in < LANES - offset, here, after)
                shifted[block] = here
            for a in range(side):
                piece = jnp.concatenate(
                    [shifted[block, lead + a : lead + a + rows, :] for block in range(blocks)],
                    axis=0,
                )
                lhs[:, a * LANES : (a + 1) * LANES] = piece.astype(jnp.bfloat16)
            response = jnp.dot(lhs[...], table[...], preferred_element_type=jnp.float32)
            for block in range(blocks):
                x = (2 * cols[block] + 1).astype(jnp.float32) / band_cols - 1.0
                matched = jnp.zeros((rows, LANES), jnp.float32)
                for k in range(kernels):
                    p = [poly_ref[(e * kernels + k) * 6 + i] for i in range(6)]
                    spatial = (p[0] + y * (p[2] + p[5] * y)) + x * ((p[1] + p[4] * y) + p[3] * x)
                    matched = matched + spatial * response[
                        block * rows : (block + 1) * rows, k * LANES : (k + 1) * LANES
                    ]
                sums[block] += weighting * matched

    in_rows = (out_row >= 0) & (out_row < band_rows)
    divisor = jnp.where(in_rows, denominator, 1.0)
    coadds = []
    for block in range(blocks):
        keep = in_rows & (cols[block] >= 0) & (cols[block] < band_cols)
        coadds.append(jnp.where(keep, sums[block] / divisor, 0.0))
    tiles = spread.shape[1] // LANES
    for tile in range(tiles):
        line = jnp.zeros((rows, LANES), jnp.float32)
        for block in range(blocks):
            low = block * step - tile * LANES
            if low + step <= 0 or low >= LANES:
                continue
            turned = pltpu.roll(coadds[block], low % LANES, 1) if low % LANES else coadds[block]
            line = jnp.where((lane >= low) & (lane < low + step), turned, line)
        spread[:, tile * LANES : (tile + 1) * LANES] = line

    def ahead(parts, tile, offset):
        if offset == 0:
            return parts[tile]
        lanes = lax.broadcasted_iota(jnp.int32, parts[tile].shape, 1)
        here = pltpu.roll(parts[tile], LANES - offset, 1)
        after = pltpu.roll(parts[tile + 1], LANES - offset, 1)
        return jnp.where(lanes < LANES - offset, here, after)

    out_tiles = tile_cols // LANES
    own = [
        spread[half : half + tile_rows, i * LANES : (i + 1) * LANES] for i in range(tiles)
    ]
    for i in range(out_tiles):
        coadd_ref[:, i * LANES : (i + 1) * LANES] = ahead(own, i, half)
    down = []
    for i in range(tiles):
        total = taps_ref[0] * spread[0:tile_rows, i * LANES : (i + 1) * LANES]
        for t in range(1, side):
            total = total + taps_ref[t] * spread[
                t : t + tile_rows, i * LANES : (i + 1) * LANES
            ]
        down.append(total)
    for i in range(out_tiles):
        total = taps_ref[0] * ahead(down, i, 0)
        for t in range(1, side):
            total = total + taps_ref[t] * ahead(down, i, t)
        detect_ref[:, i * LANES : (i + 1) * LANES] = total


def on_device(
    exposures, basis_kernels, poly_coef, exposure_weight, row_start, row_count, filter_taps
):
    members, tile_rows, tile_cols = exposures.shape
    kernels, side = basis_kernels.shape[:2]
    half = side // 2
    band_rows = tile_rows * lax.axis_size("narrow")
    band_cols = tile_cols * lax.axis_size("wide")
    step = LANES - (side - 1)
    blocks = pl.cdiv(tile_cols + 2 * half, step)
    rows = pl.cdiv(tile_rows + 2 * half, SUBLANES) * SUBLANES
    all_rows = 3 * tile_rows

    window, left, right = exchange(exposures, row_start)
    width = pl.cdiv(tile_cols + 2 * half, LANES) * LANES
    taps = basis_kernels.astype(jnp.float32).reshape(kernels * side, side)
    seed = jnp.concatenate(
        [taps[:, :1], jnp.zeros((kernels * side, step - 1), jnp.float32), taps[:, :0:-1]], axis=1
    )
    sizes = (members, kernels, side, band_rows, band_cols, tile_rows, tile_cols)
    out = jax.ShapeDtypeStruct((tile_rows, tile_cols), jnp.float32)
    scalars = pl.BlockSpec(memory_space=pltpu.SMEM)
    return pl.pallas_call(
        functools.partial(coadd_kernel, sizes),
        out_shape=(out, out),
        in_specs=[scalars] * 5 + [pl.BlockSpec(memory_space=pltpu.VMEM)] * 4,
        out_specs=(pl.BlockSpec(memory_space=pltpu.VMEM),) * 2,
        scratch_shapes=[
            pltpu.VMEM((side * LANES, kernels * LANES), jnp.bfloat16),
            pltpu.VMEM((blocks, all_rows, LANES), jnp.float32),
            pltpu.VMEM((blocks * rows, side * LANES), jnp.bfloat16),
            pltpu.VMEM((blocks, rows, LANES), jnp.float32),
            pltpu.VMEM((rows, width), jnp.float32),
        ],
        name="coadd",
    )(
        poly_coef.reshape(-1),
        exposure_weight,
        row_start,
        row_count,
        filter_taps,
        window,
        left,
        right,
        seed,
    )


def solution(mesh):
    placed = (P(None, "narrow", "wide"), P(), P(), P(), P(), P(), P())
    return jax.shard_map(
        on_device,
        mesh=mesh,
        in_specs=placed,
        out_specs=(P("narrow", "wide"), P("narrow", "wide")),
        check_vma=False,
    )
```

```python
import functools

import jax
import jax.numpy as jnp
from jax import lax
from jax.experimental import pallas as pl
from jax.experimental.pallas import tpu as pltpu
from jax.sharding import PartitionSpec as P

LANES = 128
SUBLANES = 8


MESH = pl.DeviceIdType.MESH
BF16 = jnp.bfloat16


def whole_kernel(
    sizes,
    poly_ref,
    weight_ref,
    start_ref,
    count_ref,
    taps_ref,
    x_ref,
    basis_ref,
    coadd_ref,
    detect_ref,
    window,
    edges,
    far,
    near,
    across,
    cross,
    cross_edges,
    held,
    table,
    shifted,
    lhs,
    sums,
    spread,
    turn_sent,
    turn_got,
    over_sent,
    over_got,
    end_sent,
    end_got,
    ship_sent,
    ship_got,
):
    members, kernels, side, band_rows, band_cols, tile_rows, tile_cols = sizes
    half = side // 2
    step = LANES - (side - 1)
    blocks = pl.cdiv(tile_cols + 2 * half, step)
    rows = pl.cdiv(tile_rows + 2 * half, SUBLANES) * SUBLANES
    ring = lax.axis_size("narrow") // 2
    me = lax.axis_index("narrow")
    column, columns = lax.axis_index("wide"), lax.axis_size("wide")
    second, place = me // ring, me % ring
    row_base, col_base = me * tile_rows, column * tile_cols
    has = (column > 0, column < columns - 1)

    def on_ring(turn):
        return second * ring + (place + turn + ring) % ring

    last_first = (second == 0) & (place == ring - 1)
    first_second = (second == 1) & (place == 0)
    last_second = (second == 1) & (place == ring - 1)
    other = (1 - second) * ring + place
    over_end = (1 - second) * ring + (ring - 1 - place)

    barrier = pltpu.get_barrier_semaphore()

    def greet(peer):
        pl.semaphore_signal(barrier, inc=1, device_id=peer, device_id_type=MESH)

    for peer in (on_ring(3), on_ring(-3), other):
        greet({"narrow": peer})
    for turn in (1, -1):
        greet({"narrow": on_ring(turn)})
    at_end = last_first | first_second
    count = 5 + at_end.astype(jnp.int32)

    @pl.when(at_end)
    def _():
        greet({"narrow": over_end})

    for i in range(2):
        beside = column + 2 * i - 1

        @pl.when(has[i])
        def _(beside=beside):
            greet({"wide": beside})
            for turn in (1, -1):
                greet({"narrow": on_ring(turn), "wide": beside})

        @pl.when(has[i] & at_end)
        def _(beside=beside):
            greet({"narrow": over_end, "wide": beside})

        count = count + 3 * has[i].astype(jnp.int32) + (has[i] & at_end).astype(jnp.int32)

    tap = lax.broadcasted_iota(jnp.int32, (side, LANES), 0)
    spot = lax.broadcasted_iota(jnp.int32, (side, LANES), 1)
    reverse = jnp.where((tap + spot == LANES) | (tap + spot == 0), 1.0, 0.0).astype(BF16)
    for k in range(kernels):
        seeds = jnp.dot(basis_ref[k], reverse, preferred_element_type=jnp.float32)
        for a in range(side):
            seed = jnp.broadcast_to(seeds[a : a + 1, :], (LANES, LANES))
            band = pltpu.roll(seed, 0, 1, stride=1, stride_axis=0)
            table[a * LANES : (a + 1) * LANES, k * LANES : (k + 1) * LANES] = band.astype(BF16)
    window[0, tile_rows : 2 * tile_rows, :] = x_ref[0]

    pl.semaphore_wait(barrier, count)

    def copy(src, dst, send_sem, recv_sem, peer):
        return pltpu.make_async_remote_copy(
            src_ref=src,
            dst_ref=dst,
            send_sem=send_sem,
            recv_sem=recv_sem,
            device_id=peer,
            device_id_type=MESH,
        )

    def own(e):
        return window.at[e, tile_rows : 2 * tile_rows, :]

    def turned(e, stage, i):
        src, into, by = ((x_ref, far, 3), (held, near, 1))[stage]
        slot = (2 * e + stage) * 2 + i
        peer = {"narrow": on_ring(by - 2 * by * i)}
        return copy(src.at[e], into.at[e, i], turn_sent.at[slot], turn_got.at[slot], peer)

    def over(e):
        return copy(own(e), across.at[e], over_sent.at[e], over_got.at[e], {"narrow": other})

    def lanes_of(i):
        return slice(0, LANES) if i == 0 else slice(tile_cols - LANES, tile_cols)

    def end(i):
        if i == 2:
            return copy(x_ref, cross, end_sent.at[2], end_got.at[2], {"narrow": over_end})
        return copy(
            x_ref.at[:, :, lanes_of(i)],
            cross_edges.at[1 - i],
            end_sent.at[i],
            end_got.at[i],
            {"narrow": over_end, "wide": column + 2 * i - 1},
        )

    def parcel(e, n, i, src):
        slot = (3 * e + n) * 3 + i
        where = slice(n * tile_rows, (n + 1) * tile_rows)
        peer = {"narrow": on_ring(1 - n)} if n != 1 else {}
        if i == 2:
            dst = window.at[e, where, :]
        else:
            peer["wide"] = column + 2 * i - 1
            src, dst = src.at[:, lanes_of(i)], edges.at[1 - i, e, where, :]
        return copy(src, dst, ship_sent.at[slot], ship_got.at[slot], peer)

    def each(e, src, steps, act):
        for n in steps:
            for i in (2, 0, 1):
                if i == 2:
                    if n != 1:
                        act(n, i, src)
                else:

                    @pl.when(has[i])
                    def _(n=n, i=i):
                        act(n, i, src)

    def ship(e, steps):
        if 0 in steps:

            @pl.when(last_second)
            def _():
                each(e, across.at[e], (0,), lambda n, i, src: parcel(e, n, i, src).start())

            @pl.when(jnp.logical_not(last_second))
            def _():
                each(e, own(e), (0,), lambda n, i, src: parcel(e, n, i, src).start())

        rest = tuple(n for n in steps if n)
        each(e, own(e), rest, lambda n, i, src: parcel(e, n, i, src).start())

    def arrive(e):
        for n in (0, 2):
            parcel(e, n, 2, own(e)).wait_recv()
        for i in range(2):

            @pl.when(has[1 - i])
            def _(i=i):
                for n in range(3):
                    parcel(e, n, i, own(e)).wait_recv()

    def choose(value, wanted, yes, no):
        test = jnp.full(no.shape, value, jnp.int32)
        return jnp.where(test == wanted, yes.astype(jnp.float32), no.astype(jnp.float32)).astype(BF16)

    moves = [start_ref[e] // tile_rows for e in range(members)]
    turns = [jnp.where(m > ring // 2, m - ring, m) for m in moves]
    high = [jnp.where(t >= 2, 1, jnp.where(t <= -2, -1, 0)) for t in turns]
    low = [t - 3 * h for t, h in zip(turns, high)]

    for e in range(1, members):
        for i in range(2):
            turned(e, 0, i).start()

    @pl.when(last_first)
    def _():
        over(0).start()

    ship(0, (1, 2))

    @pl.when(jnp.logical_not(last_second))
    def _():
        each(0, own(0), (0,), lambda n, i, src: parcel(0, n, i, src).start())

    @pl.when(first_second)
    def _():
        end(2).start()

    for i in range(2):

        @pl.when(first_second & has[i])
        def _(i=i):
            end(i).start()

    for e in range(1, members):
        for i in range(2):
            turned(e, 0, i).wait_recv()
        held[e] = choose(high[e], 1, far[e, 0], choose(high[e], -1, far[e, 1], x_ref[e]))
        for i in range(2):
            turned(e, 1, i).start()

    @pl.when(last_second)
    def _():
        over(0).wait_recv()
        each(0, across.at[0], (0,), lambda n, i, src: parcel(0, n, i, src).start())

    for e in range(1, members):
        for i in range(2):
            turned(e, 1, i).wait_recv()
        window[e, tile_rows : 2 * tile_rows, :] = choose(
            low[e], 1, near[e, 0], choose(low[e], -1, near[e, 1], held[e])
        )

        @pl.when(second == 0)
        def _(e=e):
            over(e).start()
            ship(e, (0, 1, 2))

    all_rows, lead = shifted.shape[1], tile_rows - 2 * half
    window_rows = row_base - tile_rows + lax.broadcasted_iota(jnp.int32, (all_rows, LANES), 0)
    lane_in = lax.broadcasted_iota(jnp.int32, (all_rows, LANES), 1)
    out_row = row_base - half + lax.broadcasted_iota(jnp.int32, (rows, LANES), 0)
    y = (2 * out_row + 1).astype(jnp.float32) / band_rows - 1.0
    lane = lax.broadcasted_iota(jnp.int32, (rows, LANES), 1)
    cols = [col_base - half + block * step + lane for block in range(blocks)]

    def match(e):
        @pl.when(last_first)
        def _():
            after = slice(2 * tile_rows, 3 * tile_rows)
            window[e, after, :] = choose(moves[e], 0, cross[e], window[e, after, :])
            for i in range(2):
                edges[i, e, after, :] = choose(
                    moves[e], 0, cross_edges[i, e], edges[i, e, after, :]
                )

        first, total = start_ref[e], count_ref[e]
        inside = (out_row >= first) & (out_row < first + total)
        weighting = weight_ref[e] * inside.astype(jnp.float32)
        valid = (window_rows >= first) & (window_rows < first + total)
        pieces = [edges[0, e]]
        for tile in range(tile_cols // LANES):
            pieces.append(window[e, :, tile * LANES : (tile + 1) * LANES])
        pieces.append(edges[1, e])
        parts = []
        for tile, piece in enumerate(pieces):
            col = lane_in + (col_base + (tile - 1) * LANES)
            keep = valid & (col >= 0) & (col < band_cols)
            parts.append(jnp.where(keep, piece.astype(jnp.float32), 0.0))
        for block in range(blocks):
            tile, offset = divmod(LANES - 2 * half + block * step, LANES)
            here = parts[tile]
            if offset:
                here = pltpu.roll(here, LANES - offset, 1)
                after = pltpu.roll(parts[tile + 1], LANES - offset, 1)
                here = jnp.where(lane_in < LANES - offset, here, after)
            shifted[block] = here
        for a in range(side):
            piece = jnp.concatenate(
                [shifted[block, lead + a : lead + a + rows, :] for block in range(blocks)], axis=0
            )
            lhs[:, a * LANES : (a + 1) * LANES] = piece.astype(BF16)
        response = jnp.dot(lhs[...], table[...], preferred_element_type=jnp.float32)
        for block in range(blocks):
            x = (2 * cols[block] + 1).astype(jnp.float32) / band_cols - 1.0
            matched = jnp.zeros((rows, LANES), jnp.float32)
            for k in range(kernels):
                p = [poly_ref[e, k, i] for i in range(6)]
                spatial = (p[0] + y * (p[2] + p[5] * y)) + x * ((p[1] + p[4] * y) + p[3] * x)
                matched = matched + spatial * response[
                    block * rows : (block + 1) * rows, k * LANES : (k + 1) * LANES
                ]
            if e == 0:
                sums[block] = weighting * matched
            else:
                sums[block] += weighting * matched
        return weighting

    @pl.when(last_first)
    def _():
        end(2).wait_recv()

    for i in range(2):

        @pl.when(last_first & has[1 - i])
        def _(i=i):
            end(i).wait_recv()

    arrive(0)
    denominator = match(0)
    for e in range(1, members):

        @pl.when(second == 1)
        def _(e=e):
            over(e).wait_recv()
            here = window[e, tile_rows : 2 * tile_rows, :].astype(jnp.float32)
            passed = jnp.full(here.shape, moves[e] - place, jnp.int32)
            chosen = jnp.where(passed > 0, across[e].astype(jnp.float32), here)
            window[e, tile_rows : 2 * tile_rows, :] = chosen.astype(BF16)
            ship(e, (0, 1, 2))

    for e in range(1, members):
        arrive(e)
        denominator = denominator + match(e)

    in_rows = (out_row >= 0) & (out_row < band_rows)
    divisor = jnp.where(in_rows, denominator, 1.0)
    coadds = []
    for block in range(blocks):
        keep = in_rows & (cols[block] >= 0) & (cols[block] < band_cols)
        coadds.append(jnp.where(keep, sums[block] / divisor, 0.0))
    tiles = spread.shape[1] // LANES
    for tile in range(tiles):
        line = jnp.zeros((rows, LANES), jnp.float32)
        for block in range(blocks):
            low = block * step - tile * LANES
            if low + step <= 0 or low >= LANES:
                continue
            rolled = pltpu.roll(coadds[block], low % LANES, 1) if low % LANES else coadds[block]
            line = jnp.where((lane >= low) & (lane < low + step), rolled, line)
        spread[:, tile * LANES : (tile + 1) * LANES] = line

    def ahead(parts, tile, offset):
        if offset == 0:
            return parts[tile]
        lanes = lax.broadcasted_iota(jnp.int32, parts[tile].shape, 1)
        here = pltpu.roll(parts[tile], LANES - offset, 1)
        after = pltpu.roll(parts[tile + 1], LANES - offset, 1)
        return jnp.where(lanes < LANES - offset, here, after)

    out_tiles = tile_cols // LANES
    mine = [
        spread[half : half + tile_rows, i * LANES : (i + 1) * LANES] for i in range(tiles)
    ]
    for i in range(out_tiles):
        coadd_ref[:, i * LANES : (i + 1) * LANES] = ahead(mine, i, half)
    down = []
    for i in range(tiles):
        total = taps_ref[0] * spread[0:tile_rows, i * LANES : (i + 1) * LANES]
        for t in range(1, side):
            total = total + taps_ref[t] * spread[
                t : t + tile_rows, i * LANES : (i + 1) * LANES
            ]
        down.append(total)
    for i in range(out_tiles):
        total = taps_ref[0] * ahead(down, i, 0)
        for t in range(1, side):
            total = total + taps_ref[t] * ahead(down, i, t)
        detect_ref[:, i * LANES : (i + 1) * LANES] = total

    for e in range(1, members):
        for stage in range(2):
            for i in range(2):
                turned(e, stage, i).wait_send()

    @pl.when(second == 0)
    def _():
        for e in range(1, members):
            over(e).wait_send()

    @pl.when(last_first)
    def _():
        over(0).wait_send()

    @pl.when(first_second)
    def _():
        end(2).wait_send()

    for i in range(2):

        @pl.when(first_second & has[i])
        def _(i=i):
            end(i).wait_send()

    for e in range(members):
        each(e, own(e), (0, 1, 2), lambda n, i, src, e=e: parcel(e, n, i, src).wait_send())


def on_device(
    exposures, basis_kernels, poly_coef, exposure_weight, row_start, row_count, filter_taps
):
    members, tile_rows, tile_cols = exposures.shape
    kernels, side = basis_kernels.shape[:2]
    half = side // 2
    band_rows = tile_rows * lax.axis_size("narrow")
    band_cols = tile_cols * lax.axis_size("wide")
    step = LANES - (side - 1)
    blocks = pl.cdiv(tile_cols + 2 * half, step)
    rows = pl.cdiv(tile_rows + 2 * half, SUBLANES) * SUBLANES
    all_rows = 3 * tile_rows
    width = pl.cdiv(tile_cols + 2 * half, LANES) * LANES
    sizes = (members, kernels, side, band_rows, band_cols, tile_rows, tile_cols)
    out = jax.ShapeDtypeStruct((tile_rows, tile_cols), jnp.float32)
    scalars = pl.BlockSpec(memory_space=pltpu.SMEM)
    vmem = pl.BlockSpec(memory_space=pltpu.VMEM)
    dma = pltpu.SemaphoreType.DMA
    return pl.pallas_call(
        functools.partial(whole_kernel, sizes),
        out_shape=(out, out),
        in_specs=[scalars] * 5 + [vmem] * 2,
        out_specs=(vmem,) * 2,
        scratch_shapes=[
            pltpu.VMEM((members, all_rows, tile_cols), BF16),
            pltpu.VMEM((2, members, all_rows, LANES), BF16),
            pltpu.VMEM((members, 2, tile_rows, tile_cols), BF16),
            pltpu.VMEM((members, 2, tile_rows, tile_cols), BF16),
            pltpu.VMEM((members, tile_rows, tile_cols), BF16),
            pltpu.VMEM((members, tile_rows, tile_cols), BF16),
            pltpu.VMEM((2, members, tile_rows, LANES), BF16),
            pltpu.VMEM((members, tile_rows, tile_cols), BF16),
            pltpu.VMEM((side * LANES, kernels * LANES), BF16),
            pltpu.VMEM((blocks, all_rows, LANES), jnp.float32),
            pltpu.VMEM((blocks * rows, side * LANES), BF16),
            pltpu.VMEM((blocks, rows, LANES), jnp.float32),
            pltpu.VMEM((rows, width), jnp.float32),
            dma((4 * members,)),
            dma((4 * members,)),
            dma((members,)),
            dma((members,)),
            dma((3,)),
            dma((3,)),
            dma((9 * members,)),
            dma((9 * members,)),
        ],
        compiler_params=pltpu.CompilerParams(collective_id=0, has_side_effects=True),
        name="whole",
    )(poly_coef, exposure_weight, row_start, row_count, filter_taps, exposures, basis_kernels)


def solution(mesh):
    placed = (P(None, "narrow", "wide"), P(), P(), P(), P(), P(), P())
    return jax.shard_map(
        on_device,
        mesh=mesh,
        in_specs=placed,
        out_specs=(P("narrow", "wide"), P("narrow", "wide")),
        check_vma=False,
    )
```

```python
import functools

import jax
import jax.numpy as jnp
from jax import lax
from jax.experimental import pallas as pl
from jax.experimental.pallas import tpu as pltpu
from jax.sharding import PartitionSpec as P

LANES = 128
SUBLANES = 8


MESH = pl.DeviceIdType.MESH
BF16 = jnp.bfloat16


def whole_kernel(
    sizes,
    poly_ref,
    weight_ref,
    start_ref,
    count_ref,
    taps_ref,
    x_ref,
    basis_ref,
    result_ref,
    window,
    edges,
    far,
    near,
    across,
    cross,
    cross_edges,
    held,
    table,
    shifted,
    lhs,
    sums,
    spread,
    turn_sent,
    turn_got,
    over_sent,
    over_got,
    end_sent,
    end_got,
    ship_sent,
    ship_got,
):
    members, kernels, side, band_rows, band_cols, tile_rows, tile_cols = sizes
    half = side // 2
    step = LANES - (side - 1)
    blocks = pl.cdiv(tile_cols + 2 * half, step)
    rows = pl.cdiv(tile_rows + 2 * half, SUBLANES) * SUBLANES
    ring = lax.axis_size("narrow") // 2
    me = lax.axis_index("narrow")
    column, columns = lax.axis_index("wide"), lax.axis_size("wide")
    second, place = me // ring, me % ring
    row_base, col_base = me * tile_rows, column * tile_cols
    has = (column > 0, column < columns - 1)

    def on_ring(turn):
        return second * ring + (place + turn + ring) % ring

    last_first = (second == 0) & (place == ring - 1)
    first_second = (second == 1) & (place == 0)
    last_second = (second == 1) & (place == ring - 1)
    other = (1 - second) * ring + place
    over_end = (1 - second) * ring + (ring - 1 - place)

    barrier = pltpu.get_barrier_semaphore()

    def greet(peer):
        pl.semaphore_signal(barrier, inc=1, device_id=peer, device_id_type=MESH)

    for peer in (on_ring(3), on_ring(-3), other):
        greet({"narrow": peer})
    for turn in (1, -1):
        greet({"narrow": on_ring(turn)})
    at_end = last_first | first_second
    count = 5 + at_end.astype(jnp.int32)

    @pl.when(at_end)
    def _():
        greet({"narrow": over_end})

    for i in range(2):
        beside = column + 2 * i - 1

        @pl.when(has[i])
        def _(beside=beside):
            greet({"wide": beside})
            for turn in (1, -1):
                greet({"narrow": on_ring(turn), "wide": beside})

        count = count + 3 * has[i].astype(jnp.int32)

    tap = lax.broadcasted_iota(jnp.int32, (side, LANES), 0)
    spot = lax.broadcasted_iota(jnp.int32, (side, LANES), 1)
    reverse = jnp.where((tap + spot == LANES) | (tap + spot == 0), 1.0, 0.0).astype(BF16)
    for k in range(kernels):
        seeds = jnp.dot(basis_ref[k], reverse, preferred_element_type=jnp.float32)
        for a in range(side):
            seed = jnp.broadcast_to(seeds[a : a + 1, :], (LANES, LANES))
            band = pltpu.roll(seed, 0, 1, stride=1, stride_axis=0)
            table[a * LANES : (a + 1) * LANES, k * LANES : (k + 1) * LANES] = band.astype(BF16)
    window[0, tile_rows : 2 * tile_rows, :] = x_ref[0]

    pl.semaphore_wait(barrier, count)

    def copy(src, dst, send_sem, recv_sem, peer):
        return pltpu.make_async_remote_copy(
            src_ref=src,
            dst_ref=dst,
            send_sem=send_sem,
            recv_sem=recv_sem,
            device_id=peer,
            device_id_type=MESH,
        )

    def own(e):
        return window.at[e, tile_rows : 2 * tile_rows, :]

    def turned(e, stage, i):
        src, into, by = ((x_ref, far, 3), (held, near, 1))[stage]
        slot = (2 * e + stage) * 2 + i
        peer = {"narrow": on_ring(by - 2 * by * i)}
        return copy(src.at[e], into.at[e, i], turn_sent.at[slot], turn_got.at[slot], peer)

    def over(e):
        return copy(own(e), across.at[e], over_sent.at[e], over_got.at[e], {"narrow": other})

    def lanes_of(i):
        return slice(0, LANES) if i == 0 else slice(tile_cols - LANES, tile_cols)

    def end(i):
        if i == 2:
            return copy(x_ref, cross, end_sent.at[2], end_got.at[2], {"narrow": over_end})
        return copy(
            cross.at[:, :, lanes_of(i)],
            cross_edges.at[1 - i],
            end_sent.at[i],
            end_got.at[i],
            {"wide": column + 2 * i - 1},
        )

    def parcel(e, n, i, src):
        slot = (3 * e + n) * 3 + i
        where = slice(n * tile_rows, (n + 1) * tile_rows)
        peer = {"narrow": on_ring(1 - n)} if n != 1 else {}
        if i == 2:
            dst = window.at[e, where, :]
        else:
            peer["wide"] = column + 2 * i - 1
            src, dst = src.at[:, lanes_of(i)], edges.at[1 - i, e, where, :]
        return copy(src, dst, ship_sent.at[slot], ship_got.at[slot], peer)

    def each(e, src, steps, act):
        for n in steps:
            for i in (2, 0, 1):
                if i == 2:
                    if n != 1:
                        act(n, i, src)
                else:

                    @pl.when(has[i])
                    def _(n=n, i=i):
                        act(n, i, src)

    def ship(e, steps):
        if 0 in steps:

            @pl.when(last_second)
            def _():
                each(e, across.at[e], (0,), lambda n, i, src: parcel(e, n, i, src).start())

            @pl.when(jnp.logical_not(last_second))
            def _():
                each(e, own(e), (0,), lambda n, i, src: parcel(e, n, i, src).start())

        rest = tuple(n for n in steps if n)
        each(e, own(e), rest, lambda n, i, src: parcel(e, n, i, src).start())

    def arrive(e):
        for n in (0, 2):
            parcel(e, n, 2, own(e)).wait_recv()
        for i in range(2):

            @pl.when(has[1 - i])
            def _(i=i):
                for n in range(3):
                    parcel(e, n, i, own(e)).wait_recv()

    def choose(value, wanted, yes, no):
        test = jnp.full(no.shape, value, jnp.int32)
        return jnp.where(test == wanted, yes.astype(jnp.float32), no.astype(jnp.float32)).astype(BF16)

    moves = [start_ref[e] // tile_rows for e in range(members)]
    turns = [jnp.where(m > ring // 2, m - ring, m) for m in moves]
    high = [jnp.where(t >= 2, 1, jnp.where(t <= -2, -1, 0)) for t in turns]
    low = [t - 3 * h for t, h in zip(turns, high)]

    for e in range(1, members):
        for i in range(2):
            turned(e, 0, i).start()

    @pl.when(last_first)
    def _():
        over(0).start()

    ship(0, (1, 2))

    @pl.when(jnp.logical_not(last_second))
    def _():
        each(0, own(0), (0,), lambda n, i, src: parcel(0, n, i, src).start())

    @pl.when(first_second)
    def _():
        end(2).start()

    for e in range(1, members):
        for i in range(2):
            turned(e, 0, i).wait_recv()
        held[e] = choose(high[e], 1, far[e, 0], choose(high[e], -1, far[e, 1], x_ref[e]))
        for i in range(2):
            turned(e, 1, i).start()

    @pl.when(last_second)
    def _():
        over(0).wait_recv()
        each(0, across.at[0], (0,), lambda n, i, src: parcel(0, n, i, src).start())

    for e in range(1, members):
        for i in range(2):
            turned(e, 1, i).wait_recv()
        window[e, tile_rows : 2 * tile_rows, :] = choose(
            low[e], 1, near[e, 0], choose(low[e], -1, near[e, 1], held[e])
        )

        @pl.when(second == 0)
        def _(e=e):
            over(e).start()
            ship(e, (0, 1, 2))

    all_rows, lead = shifted.shape[1], tile_rows - 2 * half
    window_rows = row_base - tile_rows + lax.broadcasted_iota(jnp.int32, (all_rows, LANES), 0)
    lane_in = lax.broadcasted_iota(jnp.int32, (all_rows, LANES), 1)
    out_row = row_base - half + lax.broadcasted_iota(jnp.int32, (rows, LANES), 0)
    y = (2 * out_row + 1).astype(jnp.float32) / band_rows - 1.0
    lane = lax.broadcasted_iota(jnp.int32, (rows, LANES), 1)
    cols = [col_base - half + block * step + lane for block in range(blocks)]

    def match(e):
        @pl.when(last_first)
        def _():
            after = slice(2 * tile_rows, 3 * tile_rows)
            window[e, after, :] = choose(moves[e], 0, cross[e], window[e, after, :])
            for i in range(2):
                edges[i, e, after, :] = choose(
                    moves[e], 0, cross_edges[i, e], edges[i, e, after, :]
                )

        first, total = start_ref[e], count_ref[e]
        inside = (out_row >= first) & (out_row < first + total)
        weighting = weight_ref[e] * inside.astype(jnp.float32)
        valid = (window_rows >= first) & (window_rows < first + total)
        pieces = [edges[0, e]]
        for tile in range(tile_cols // LANES):
            pieces.append(window[e, :, tile * LANES : (tile + 1) * LANES])
        pieces.append(edges[1, e])
        parts = []
        for tile, piece in enumerate(pieces):
            col = lane_in + (col_base + (tile - 1) * LANES)
            keep = valid & (col >= 0) & (col < band_cols)
            parts.append(jnp.where(keep, piece.astype(jnp.float32), 0.0))
        for block in range(blocks):
            tile, offset = divmod(LANES - 2 * half + block * step, LANES)
            here = parts[tile]
            if offset:
                here = pltpu.roll(here, LANES - offset, 1)
                after = pltpu.roll(parts[tile + 1], LANES - offset, 1)
                here = jnp.where(lane_in < LANES - offset, here, after)
            shifted[block] = here
        for a in range(side):
            piece = jnp.concatenate(
                [shifted[block, lead + a : lead + a + rows, :] for block in range(blocks)], axis=0
            )
            lhs[:, a * LANES : (a + 1) * LANES] = piece.astype(BF16)
        response = jnp.dot(lhs[...], table[...], preferred_element_type=jnp.float32)
        for block in range(blocks):
            x = (2 * cols[block] + 1).astype(jnp.float32) / band_cols - 1.0
            matched = jnp.zeros((rows, LANES), jnp.float32)
            for k in range(kernels):
                p = [poly_ref[k, e, i] for i in range(6)]
                spatial = (p[0] + y * (p[2] + p[5] * y)) + x * ((p[1] + p[4] * y) + p[3] * x)
                matched = matched + spatial * response[
                    block * rows : (block + 1) * rows, k * LANES : (k + 1) * LANES
                ]
            if e == 0:
                sums[block] = weighting * matched
            else:
                sums[block] += weighting * matched
        return weighting

    @pl.when(last_first)
    def _():
        end(2).wait_recv()

    for i in range(2):

        @pl.when(last_first & has[i])
        def _(i=i):
            end(i).start()

    for i in range(2):

        @pl.when(last_first & has[1 - i])
        def _(i=i):
            end(i).wait_recv()

    arrive(0)
    denominator = match(0)
    for e in range(1, members):

        @pl.when(second == 1)
        def _(e=e):
            over(e).wait_recv()
            here = window[e, tile_rows : 2 * tile_rows, :].astype(jnp.float32)
            passed = jnp.full(here.shape, moves[e] - place, jnp.int32)
            chosen = jnp.where(passed > 0, across[e].astype(jnp.float32), here)
            window[e, tile_rows : 2 * tile_rows, :] = chosen.astype(BF16)
            ship(e, (0, 1, 2))

    for e in range(1, members):
        arrive(e)
        denominator = denominator + match(e)

    in_rows = (out_row >= 0) & (out_row < band_rows)
    divisor = jnp.where(in_rows, denominator, 1.0)
    coadds = []
    for block in range(blocks):
        keep = in_rows & (cols[block] >= 0) & (cols[block] < band_cols)
        coadds.append(jnp.where(keep, sums[block] / divisor, 0.0))
    tiles = spread.shape[1] // LANES
    for tile in range(tiles):
        line = jnp.zeros((rows, LANES), jnp.float32)
        for block in range(blocks):
            low = block * step - tile * LANES
            if low + step <= 0 or low >= LANES:
                continue
            rolled = pltpu.roll(coadds[block], low % LANES, 1) if low % LANES else coadds[block]
            line = jnp.where((lane >= low) & (lane < low + step), rolled, line)
        spread[:, tile * LANES : (tile + 1) * LANES] = line

    def ahead(parts, tile, offset):
        if offset == 0:
            return parts[tile]
        lanes = lax.broadcasted_iota(jnp.int32, parts[tile].shape, 1)
        here = pltpu.roll(parts[tile], LANES - offset, 1)
        after = pltpu.roll(parts[tile + 1], LANES - offset, 1)
        return jnp.where(lanes < LANES - offset, here, after)

    out_tiles = tile_cols // LANES
    mine = [
        spread[half : half + tile_rows, i * LANES : (i + 1) * LANES] for i in range(tiles)
    ]
    for i in range(out_tiles):
        result_ref[0, :, i * LANES : (i + 1) * LANES] = ahead(mine, i, half)
    down = []
    for i in range(tiles):
        total = taps_ref[0] * spread[0:tile_rows, i * LANES : (i + 1) * LANES]
        for t in range(1, side):
            total = total + taps_ref[t] * spread[
                t : t + tile_rows, i * LANES : (i + 1) * LANES
            ]
        down.append(total)
    for i in range(out_tiles):
        total = taps_ref[0] * ahead(down, i, 0)
        for t in range(1, side):
            total = total + taps_ref[t] * ahead(down, i, t)
        result_ref[1, :, i * LANES : (i + 1) * LANES] = total

    for e in range(1, members):
        for stage in range(2):
            for i in range(2):
                turned(e, stage, i).wait_send()

    @pl.when(second == 0)
    def _():
        for e in range(1, members):
            over(e).wait_send()

    @pl.when(last_first)
    def _():
        over(0).wait_send()

    @pl.when(first_second)
    def _():
        end(2).wait_send()

    for i in range(2):

        @pl.when(last_first & has[i])
        def _(i=i):
            end(i).wait_send()

    for e in range(members):
        each(e, own(e), (0, 1, 2), lambda n, i, src, e=e: parcel(e, n, i, src).wait_send())


def on_device(
    exposures, basis_kernels, poly_coef, exposure_weight, row_start, row_count, filter_taps
):
    members, tile_rows, tile_cols = exposures.shape
    kernels, side = basis_kernels.shape[:2]
    half = side // 2
    band_rows = tile_rows * lax.axis_size("narrow")
    band_cols = tile_cols * lax.axis_size("wide")
    step = LANES - (side - 1)
    blocks = pl.cdiv(tile_cols + 2 * half, step)
    rows = pl.cdiv(tile_rows + 2 * half, SUBLANES) * SUBLANES
    all_rows = 3 * tile_rows
    width = pl.cdiv(tile_cols + 2 * half, LANES) * LANES
    sizes = (members, kernels, side, band_rows, band_cols, tile_rows, tile_cols)
    out = jax.ShapeDtypeStruct((2, tile_rows, tile_cols), jnp.float32)
    scalars = pl.BlockSpec(memory_space=pltpu.SMEM)
    vmem = pl.BlockSpec(memory_space=pltpu.VMEM)
    dma = pltpu.SemaphoreType.DMA
    results = pl.pallas_call(
        functools.partial(whole_kernel, sizes),
        out_shape=out,
        in_specs=[scalars] * 5 + [vmem] * 2,
        out_specs=vmem,
        scratch_shapes=[
            pltpu.VMEM((members, all_rows, tile_cols), BF16),
            pltpu.VMEM((2, members, all_rows, LANES), BF16),
            pltpu.VMEM((members, 2, tile_rows, tile_cols), BF16),
            pltpu.VMEM((members, 2, tile_rows, tile_cols), BF16),
            pltpu.VMEM((members, tile_rows, tile_cols), BF16),
            pltpu.VMEM((members, tile_rows, tile_cols), BF16),
            pltpu.VMEM((2, members, tile_rows, LANES), BF16),
            pltpu.VMEM((members, tile_rows, tile_cols), BF16),
            pltpu.VMEM((side * LANES, kernels * LANES), BF16),
            pltpu.VMEM((blocks, all_rows, LANES), jnp.float32),
            pltpu.VMEM((blocks * rows, side * LANES), BF16),
            pltpu.VMEM((blocks, rows, LANES), jnp.float32),
            pltpu.VMEM((rows, width), jnp.float32),
            dma((4 * members,)),
            dma((4 * members,)),
            dma((members,)),
            dma((members,)),
            dma((3,)),
            dma((3,)),
            dma((9 * members,)),
            dma((9 * members,)),
        ],
        compiler_params=pltpu.CompilerParams(collective_id=0, has_side_effects=True),
        name="whole",
    )(poly_coef.transpose(1, 0, 2), exposure_weight, row_start, row_count, filter_taps, exposures, basis_kernels)
    return results[0], results[1]


def solution(mesh):
    placed = (P(None, "narrow", "wide"), P(), P(), P(), P(), P(), P())
    return jax.shard_map(
        on_device,
        mesh=mesh,
        in_specs=placed,
        out_specs=(P("narrow", "wide"), P("narrow", "wide")),
        check_vma=False,
    )
```

```python
import functools

import jax
import jax.numpy as jnp
from jax import lax
from jax.experimental import pallas as pl
from jax.experimental.pallas import tpu as pltpu
from jax.sharding import PartitionSpec as P

LANES = 128
SUBLANES = 8


MESH = pl.DeviceIdType.MESH
BF16 = jnp.bfloat16


def whole_kernel(
    sizes,
    poly_ref,
    weight_ref,
    start_ref,
    count_ref,
    taps_ref,
    x_hbm,
    basis_ref,
    result_ref,
    x_ref,
    window,
    edges,
    far,
    near,
    across,
    cross,
    cross_edges,
    held,
    table,
    shifted,
    lhs,
    sums,
    spread,
    turn_sent,
    turn_got,
    over_sent,
    over_got,
    end_sent,
    end_got,
    ship_sent,
    ship_got,
    fetched,
):
    members, kernels, side, band_rows, band_cols, tile_rows, tile_cols = sizes
    half = side // 2
    step = LANES - (side - 1)
    blocks = pl.cdiv(tile_cols + 2 * half, step)
    rows = pl.cdiv(tile_rows + 2 * half, SUBLANES) * SUBLANES
    ring = lax.axis_size("narrow") // 2
    me = lax.axis_index("narrow")
    column, columns = lax.axis_index("wide"), lax.axis_size("wide")
    second, place = me // ring, me % ring
    row_base, col_base = me * tile_rows, column * tile_cols
    has = (column > 0, column < columns - 1)

    def on_ring(turn):
        return second * ring + (place + turn + ring) % ring

    last_first = (second == 0) & (place == ring - 1)
    first_second = (second == 1) & (place == 0)
    last_second = (second == 1) & (place == ring - 1)
    other = (1 - second) * ring + place
    over_end = (1 - second) * ring + (ring - 1 - place)

    fetch = pltpu.make_async_copy(x_hbm, x_ref, fetched)
    fetch.start()
    barrier = pltpu.get_barrier_semaphore()

    def greet(peer):
        pl.semaphore_signal(barrier, inc=1, device_id=peer, device_id_type=MESH)

    for peer in (on_ring(3), on_ring(-3), other):
        greet({"narrow": peer})
    for turn in (1, -1):
        greet({"narrow": on_ring(turn)})
    at_end = last_first | first_second
    count = 5 + at_end.astype(jnp.int32)

    @pl.when(at_end)
    def _():
        greet({"narrow": over_end})

    for i in range(2):
        beside = column + 2 * i - 1

        @pl.when(has[i])
        def _(beside=beside):
            greet({"wide": beside})
            for turn in (1, -1):
                greet({"narrow": on_ring(turn), "wide": beside})

        count = count + 3 * has[i].astype(jnp.int32)

    fetch.wait()
    pl.semaphore_wait(barrier, count)

    def copy(src, dst, send_sem, recv_sem, peer):
        return pltpu.make_async_remote_copy(
            src_ref=src,
            dst_ref=dst,
            send_sem=send_sem,
            recv_sem=recv_sem,
            device_id=peer,
            device_id_type=MESH,
        )

    def own(e):
        return window.at[e, tile_rows : 2 * tile_rows, :]

    def turned(e, stage, i):
        src, into, by = ((x_ref, far, 3), (held, near, 1))[stage]
        slot = (2 * e + stage) * 2 + i
        peer = {"narrow": on_ring(by - 2 * by * i)}
        return copy(src.at[e], into.at[e, i], turn_sent.at[slot], turn_got.at[slot], peer)

    def over(e):
        return copy(own(e), across.at[e], over_sent.at[e], over_got.at[e], {"narrow": other})

    def lanes_of(i):
        return slice(0, LANES) if i == 0 else slice(tile_cols - LANES, tile_cols)

    def end(i):
        if i == 2:
            return copy(x_ref, cross, end_sent.at[2], end_got.at[2], {"narrow": over_end})
        return copy(
            cross.at[:, :, lanes_of(i)],
            cross_edges.at[1 - i],
            end_sent.at[i],
            end_got.at[i],
            {"wide": column + 2 * i - 1},
        )

    def parcel(e, n, i, src):
        slot = (3 * e + n) * 3 + i
        where = slice(n * tile_rows, (n + 1) * tile_rows)
        peer = {"narrow": on_ring(1 - n)} if n != 1 else {}
        if i == 2:
            dst = window.at[e, where, :]
        else:
            peer["wide"] = column + 2 * i - 1
            src, dst = src.at[:, lanes_of(i)], edges.at[1 - i, e, where, :]
        return copy(src, dst, ship_sent.at[slot], ship_got.at[slot], peer)

    def each(e, src, steps, act):
        for n in steps:
            for i in (2, 0, 1):
                if i == 2:
                    if n != 1:
                        act(n, i, src)
                else:

                    @pl.when(has[i])
                    def _(n=n, i=i):
                        act(n, i, src)

    def ship(e, steps):
        if 0 in steps:

            @pl.when(last_second)
            def _():
                each(e, across.at[e], (0,), lambda n, i, src: parcel(e, n, i, src).start())

            @pl.when(jnp.logical_not(last_second))
            def _():
                each(e, own(e), (0,), lambda n, i, src: parcel(e, n, i, src).start())

        rest = tuple(n for n in steps if n)
        each(e, own(e), rest, lambda n, i, src: parcel(e, n, i, src).start())

    def arrive(e):
        for n in (0, 2):
            parcel(e, n, 2, own(e)).wait_recv()
        for i in range(2):

            @pl.when(has[1 - i])
            def _(i=i):
                for n in range(3):
                    parcel(e, n, i, own(e)).wait_recv()

    def choose(value, wanted, yes, no):
        test = jnp.full(no.shape, value, jnp.int32)
        return jnp.where(test == wanted, yes.astype(jnp.float32), no.astype(jnp.float32)).astype(BF16)

    moves = [start_ref[e] // tile_rows for e in range(members)]
    turns = [jnp.where(m > ring // 2, m - ring, m) for m in moves]
    high = [jnp.where(t >= 2, 1, jnp.where(t <= -2, -1, 0)) for t in turns]
    low = [t - 3 * h for t, h in zip(turns, high)]

    for e in range(1, members):
        for i in range(2):
            turned(e, 0, i).start()

    window[0, tile_rows : 2 * tile_rows, :] = x_ref[0]
    @pl.when(last_first)
    def _():
        over(0).start()

    ship(0, (1, 2))

    @pl.when(jnp.logical_not(last_second))
    def _():
        each(0, own(0), (0,), lambda n, i, src: parcel(0, n, i, src).start())

    @pl.when(first_second)
    def _():
        end(2).start()

    tap = lax.broadcasted_iota(jnp.int32, (side, LANES), 0)
    spot = lax.broadcasted_iota(jnp.int32, (side, LANES), 1)
    reverse = jnp.where((tap + spot == LANES) | (tap + spot == 0), 1.0, 0.0).astype(BF16)
    for k in range(kernels):
        seeds = jnp.dot(basis_ref[k], reverse, preferred_element_type=jnp.float32)
        for a in range(side):
            seed = jnp.broadcast_to(seeds[a : a + 1, :], (LANES, LANES))
            band = pltpu.roll(seed, 0, 1, stride=1, stride_axis=0)
            table[a * LANES : (a + 1) * LANES, k * LANES : (k + 1) * LANES] = band.astype(BF16)

    for e in range(1, members):
        for i in range(2):
            turned(e, 0, i).wait_recv()
        held[e] = choose(high[e], 1, far[e, 0], choose(high[e], -1, far[e, 1], x_ref[e]))
        for i in range(2):
            turned(e, 1, i).start()

    @pl.when(last_second)
    def _():
        over(0).wait_recv()
        each(0, across.at[0], (0,), lambda n, i, src: parcel(0, n, i, src).start())

    for e in range(1, members):
        for i in range(2):
            turned(e, 1, i).wait_recv()
        window[e, tile_rows : 2 * tile_rows, :] = choose(
            low[e], 1, near[e, 0], choose(low[e], -1, near[e, 1], held[e])
        )

        @pl.when(second == 0)
        def _(e=e):
            over(e).start()
            ship(e, (0, 1, 2))

    all_rows, lead = shifted.shape[1], tile_rows - 2 * half
    window_rows = row_base - tile_rows + lax.broadcasted_iota(jnp.int32, (all_rows, LANES), 0)
    lane_in = lax.broadcasted_iota(jnp.int32, (all_rows, LANES), 1)
    out_row = row_base - half + lax.broadcasted_iota(jnp.int32, (rows, LANES), 0)
    y = (2 * out_row + 1).astype(jnp.float32) / band_rows - 1.0
    lane = lax.broadcasted_iota(jnp.int32, (rows, LANES), 1)
    cols = [col_base - half + block * step + lane for block in range(blocks)]

    def match(e):
        @pl.when(last_first)
        def _():
            after = slice(2 * tile_rows, 3 * tile_rows)
            window[e, after, :] = choose(moves[e], 0, cross[e], window[e, after, :])
            for i in range(2):
                edges[i, e, after, :] = choose(
                    moves[e], 0, cross_edges[i, e], edges[i, e, after, :]
                )

        first, total = start_ref[e], count_ref[e]
        inside = (out_row >= first) & (out_row < first + total)
        weighting = weight_ref[e] * inside.astype(jnp.float32)
        valid = (window_rows >= first) & (window_rows < first + total)
        pieces = [edges[0, e]]
        for tile in range(tile_cols // LANES):
            pieces.append(window[e, :, tile * LANES : (tile + 1) * LANES])
        pieces.append(edges[1, e])
        parts = []
        for tile, piece in enumerate(pieces):
            col = lane_in + (col_base + (tile - 1) * LANES)
            keep = valid & (col >= 0) & (col < band_cols)
            parts.append(jnp.where(keep, piece.astype(jnp.float32), 0.0))
        for block in range(blocks):
            tile, offset = divmod(LANES - 2 * half + block * step, LANES)
            here = parts[tile]
            if offset:
                here = pltpu.roll(here, LANES - offset, 1)
                after = pltpu.roll(parts[tile + 1], LANES - offset, 1)
                here = jnp.where(lane_in < LANES - offset, here, after)
            shifted[block] = here
        for a in range(side):
            piece = jnp.concatenate(
                [shifted[block, lead + a : lead + a + rows, :] for block in range(blocks)], axis=0
            )
            lhs[:, a * LANES : (a + 1) * LANES] = piece.astype(BF16)
        response = jnp.dot(lhs[...], table[...], preferred_element_type=jnp.float32)
        for block in range(blocks):
            x = (2 * cols[block] + 1).astype(jnp.float32) / band_cols - 1.0
            matched = jnp.zeros((rows, LANES), jnp.float32)
            for k in range(kernels):
                p = [poly_ref[k, e, i] for i in range(6)]
                spatial = (p[0] + y * (p[2] + p[5] * y)) + x * ((p[1] + p[4] * y) + p[3] * x)
                matched = matched + spatial * response[
                    block * rows : (block + 1) * rows, k * LANES : (k + 1) * LANES
                ]
            if e == 0:
                sums[block] = weighting * matched
            else:
                sums[block] += weighting * matched
    @pl.when(last_first)
    def _():
        end(2).wait_recv()

    for i in range(2):

        @pl.when(last_first & has[i])
        def _(i=i):
            end(i).start()

    for i in range(2):

        @pl.when(last_first & has[1 - i])
        def _(i=i):
            end(i).wait_recv()

    arrive(0)
    match(0)
    for e in range(1, members):

        @pl.when(second == 1)
        def _(e=e):
            over(e).wait_recv()
            here = window[e, tile_rows : 2 * tile_rows, :].astype(jnp.float32)
            passed = jnp.full(here.shape, moves[e] - place, jnp.int32)
            chosen = jnp.where(passed > 0, across[e].astype(jnp.float32), here)
            window[e, tile_rows : 2 * tile_rows, :] = chosen.astype(BF16)
            ship(e, (0, 1, 2))

    denominator = jnp.zeros((rows, LANES), jnp.float32)
    for e in range(members):
        inside = (out_row >= start_ref[e]) & (out_row < start_ref[e] + count_ref[e])
        denominator = denominator + weight_ref[e] * inside.astype(jnp.float32)
    in_rows = (out_row >= 0) & (out_row < band_rows)
    inverse = 1.0 / jnp.where(in_rows, denominator, 1.0)

    for e in range(1, members):
        arrive(e)
        match(e)

    coadds = []
    for block in range(blocks):
        keep = in_rows & (cols[block] >= 0) & (cols[block] < band_cols)
        coadds.append(jnp.where(keep, sums[block] * inverse, 0.0))
    tiles = spread.shape[1] // LANES
    for tile in range(tiles):
        line = jnp.zeros((rows, LANES), jnp.float32)
        for block in range(blocks):
            low = block * step - tile * LANES
            if low + step <= 0 or low >= LANES:
                continue
            rolled = pltpu.roll(coadds[block], low % LANES, 1) if low % LANES else coadds[block]
            line = jnp.where((lane >= low) & (lane < low + step), rolled, line)
        spread[:, tile * LANES : (tile + 1) * LANES] = line

    def ahead(parts, tile, offset):
        if offset == 0:
            return parts[tile]
        lanes = lax.broadcasted_iota(jnp.int32, parts[tile].shape, 1)
        here = pltpu.roll(parts[tile], LANES - offset, 1)
        after = pltpu.roll(parts[tile + 1], LANES - offset, 1)
        return jnp.where(lanes < LANES - offset, here, after)

    out_tiles = tile_cols // LANES
    mine = [
        spread[half : half + tile_rows, i * LANES : (i + 1) * LANES] for i in range(tiles)
    ]
    for i in range(out_tiles):
        result_ref[0, :, i * LANES : (i + 1) * LANES] = ahead(mine, i, half)
    down = []
    for i in range(tiles):
        total = taps_ref[0] * spread[0:tile_rows, i * LANES : (i + 1) * LANES]
        for t in range(1, side):
            total = total + taps_ref[t] * spread[
                t : t + tile_rows, i * LANES : (i + 1) * LANES
            ]
        down.append(total)
    totals = [taps_ref[0] * down[i] for i in range(out_tiles)]
    lanes = lax.broadcasted_iota(jnp.int32, down[0].shape, 1)
    for t in range(1, side):
        rolled = [pltpu.roll(part, LANES - t, 1) for part in down]
        for i in range(out_tiles):
            here = jnp.where(lanes < LANES - t, rolled[i], rolled[i + 1])
            totals[i] = totals[i] + taps_ref[t] * here
    for i in range(out_tiles):
        result_ref[1, :, i * LANES : (i + 1) * LANES] = totals[i]

    for e in range(1, members):
        for stage in range(2):
            for i in range(2):
                turned(e, stage, i).wait_send()

    @pl.when(second == 0)
    def _():
        for e in range(1, members):
            over(e).wait_send()

    @pl.when(last_first)
    def _():
        over(0).wait_send()

    @pl.when(first_second)
    def _():
        end(2).wait_send()

    for i in range(2):

        @pl.when(last_first & has[i])
        def _(i=i):
            end(i).wait_send()

    for e in range(members):
        each(e, own(e), (0, 1, 2), lambda n, i, src, e=e: parcel(e, n, i, src).wait_send())


def on_device(
    exposures, basis_kernels, poly_coef, exposure_weight, row_start, row_count, filter_taps
):
    members, tile_rows, tile_cols = exposures.shape
    kernels, side = basis_kernels.shape[:2]
    half = side // 2
    band_rows = tile_rows * lax.axis_size("narrow")
    band_cols = tile_cols * lax.axis_size("wide")
    step = LANES - (side - 1)
    blocks = pl.cdiv(tile_cols + 2 * half, step)
    rows = pl.cdiv(tile_rows + 2 * half, SUBLANES) * SUBLANES
    all_rows = 3 * tile_rows
    width = pl.cdiv(tile_cols + 2 * half, LANES) * LANES
    sizes = (members, kernels, side, band_rows, band_cols, tile_rows, tile_cols)
    out = jax.ShapeDtypeStruct((2, tile_rows, tile_cols), jnp.float32)
    scalars = pl.BlockSpec(memory_space=pltpu.SMEM)
    vmem = pl.BlockSpec(memory_space=pltpu.VMEM)
    dma = pltpu.SemaphoreType.DMA
    results = pl.pallas_call(
        functools.partial(whole_kernel, sizes),
        out_shape=out,
        in_specs=[scalars] * 5 + [pl.BlockSpec(memory_space=pl.ANY), vmem],
        out_specs=vmem,
        scratch_shapes=[
            pltpu.VMEM((members, tile_rows, tile_cols), BF16),
            pltpu.VMEM((members, all_rows, tile_cols), BF16),
            pltpu.VMEM((2, members, all_rows, LANES), BF16),
            pltpu.VMEM((members, 2, tile_rows, tile_cols), BF16),
            pltpu.VMEM((members, 2, tile_rows, tile_cols), BF16),
            pltpu.VMEM((members, tile_rows, tile_cols), BF16),
            pltpu.VMEM((members, tile_rows, tile_cols), BF16),
            pltpu.VMEM((2, members, tile_rows, LANES), BF16),
            pltpu.VMEM((members, tile_rows, tile_cols), BF16),
            pltpu.VMEM((side * LANES, kernels * LANES), BF16),
            pltpu.VMEM((blocks, all_rows, LANES), jnp.float32),
            pltpu.VMEM((blocks * rows, side * LANES), BF16),
            pltpu.VMEM((blocks, rows, LANES), jnp.float32),
            pltpu.VMEM((rows, width), jnp.float32),
            dma((4 * members,)),
            dma((4 * members,)),
            dma((members,)),
            dma((members,)),
            dma((3,)),
            dma((3,)),
            dma((9 * members,)),
            dma((9 * members,)),
            dma,
        ],
        compiler_params=pltpu.CompilerParams(collective_id=0, has_side_effects=True),
        name="whole",
    )(poly_coef.transpose(1, 0, 2), exposure_weight, row_start, row_count, filter_taps, exposures, basis_kernels)
    return results[0], results[1]


def solution(mesh):
    placed = (P(None, "narrow", "wide"), P(), P(), P(), P(), P(), P())
    return jax.shard_map(
        on_device,
        mesh=mesh,
        in_specs=placed,
        out_specs=(P("narrow", "wide"), P("narrow", "wide")),
        check_vma=False,
    )
```

```python
import functools

import jax
import jax.numpy as jnp
from jax import lax
from jax.experimental import pallas as pl
from jax.experimental.pallas import tpu as pltpu
from jax.sharding import PartitionSpec as P

LANES = 128
SUBLANES = 8


MESH = pl.DeviceIdType.MESH
BF16 = jnp.bfloat16


def whole_kernel(
    sizes,
    poly_ref,
    weight_ref,
    start_ref,
    count_ref,
    taps_ref,
    x_hbm,
    basis_ref,
    result_ref,
    x_ref,
    window,
    edges,
    far,
    near,
    across,
    cross,
    cross_edges,
    held,
    table,
    shifted,
    lhs,
    sums,
    spread,
    turn_sent,
    turn_got,
    over_sent,
    over_got,
    end_sent,
    end_got,
    ship_sent,
    ship_got,
    fetched,
):
    members, kernels, side, band_rows, band_cols, tile_rows, tile_cols = sizes
    half = side // 2
    step = LANES - (side - 1)
    blocks = pl.cdiv(tile_cols + 2 * half, step)
    rows = pl.cdiv(tile_rows + 2 * half, SUBLANES) * SUBLANES
    ring = lax.axis_size("narrow") // 2
    me = lax.axis_index("narrow")
    column, columns = lax.axis_index("wide"), lax.axis_size("wide")
    second, place = me // ring, me % ring
    row_base, col_base = me * tile_rows, column * tile_cols
    has = (column > 0, column < columns - 1)

    def on_ring(turn):
        return second * ring + (place + turn + ring) % ring

    last_first = (second == 0) & (place == ring - 1)
    first_second = (second == 1) & (place == 0)
    last_second = (second == 1) & (place == ring - 1)
    other = (1 - second) * ring + place
    over_end = (1 - second) * ring + (ring - 1 - place)

    fetch = pltpu.make_async_copy(x_hbm, x_ref, fetched)
    fetch.start()
    barrier = pltpu.get_barrier_semaphore()

    def greet(peer):
        pl.semaphore_signal(barrier, inc=1, device_id=peer, device_id_type=MESH)

    for peer in (on_ring(3), on_ring(-3), other):
        greet({"narrow": peer})
    for turn in (1, -1):
        greet({"narrow": on_ring(turn)})
    at_end = last_first | first_second
    count = 5 + at_end.astype(jnp.int32)

    @pl.when(at_end)
    def _():
        greet({"narrow": over_end})

    for i in range(2):
        beside = column + 2 * i - 1

        @pl.when(has[i])
        def _(beside=beside):
            greet({"wide": beside})
            for turn in (1, -1):
                greet({"narrow": on_ring(turn), "wide": beside})

        count = count + 3 * has[i].astype(jnp.int32)

    fetch.wait()
    pl.semaphore_wait(barrier, count)

    def copy(src, dst, send_sem, recv_sem, peer):
        return pltpu.make_async_remote_copy(
            src_ref=src,
            dst_ref=dst,
            send_sem=send_sem,
            recv_sem=recv_sem,
            device_id=peer,
            device_id_type=MESH,
        )

    def own(e):
        return window.at[e, tile_rows : 2 * tile_rows, :]

    part = tile_rows // 2

    def rows_of(h):
        return slice(h * part, (h + 1) * part)

    def own_rows(h):
        return slice(tile_rows + h * part, tile_rows + (h + 1) * part)

    def turned(e, stage, i, h):
        src, into, by = ((x_ref, far, 3), (held, near, 1))[stage]
        slot = ((2 * e + stage) * 2 + i) * 2 + h
        peer = {"narrow": on_ring(by - 2 * by * i)}
        return copy(
            src.at[e, rows_of(h)],
            into.at[e, i, rows_of(h)],
            turn_sent.at[slot],
            turn_got.at[slot],
            peer,
        )

    def over(e, h):
        slot = 2 * e + h
        return copy(
            window.at[e, own_rows(h), :],
            across.at[e, rows_of(h)],
            over_sent.at[slot],
            over_got.at[slot],
            {"narrow": other},
        )

    def lanes_of(i):
        return slice(0, LANES) if i == 0 else slice(tile_cols - LANES, tile_cols)

    def end(i):
        if i == 2:
            return copy(x_ref, cross, end_sent.at[2], end_got.at[2], {"narrow": over_end})
        return copy(
            cross.at[:, :, lanes_of(i)],
            cross_edges.at[1 - i],
            end_sent.at[i],
            end_got.at[i],
            {"wide": column + 2 * i - 1},
        )

    def parcel(e, n, i, src):
        slot = (3 * e + n) * 3 + i
        where = slice(n * tile_rows, (n + 1) * tile_rows)
        peer = {"narrow": on_ring(1 - n)} if n != 1 else {}
        if i == 2:
            dst = window.at[e, where, :]
        else:
            peer["wide"] = column + 2 * i - 1
            src, dst = src.at[:, lanes_of(i)], edges.at[1 - i, e, where, :]
        return copy(src, dst, ship_sent.at[slot], ship_got.at[slot], peer)

    def each(e, src, steps, act):
        for n in steps:
            for i in (2, 0, 1):
                if i == 2:
                    if n != 1:
                        act(n, i, src)
                else:

                    @pl.when(has[i])
                    def _(n=n, i=i):
                        act(n, i, src)

    def ship(e, steps):
        if 0 in steps:

            @pl.when(last_second)
            def _():
                each(e, across.at[e], (0,), lambda n, i, src: parcel(e, n, i, src).start())

            @pl.when(jnp.logical_not(last_second))
            def _():
                each(e, own(e), (0,), lambda n, i, src: parcel(e, n, i, src).start())

        rest = tuple(n for n in steps if n)
        each(e, own(e), rest, lambda n, i, src: parcel(e, n, i, src).start())

    def arrive(e):
        for n in (0, 2):
            parcel(e, n, 2, own(e)).wait_recv()
        for i in range(2):

            @pl.when(has[1 - i])
            def _(i=i):
                for n in range(3):
                    parcel(e, n, i, own(e)).wait_recv()

    def choose(value, wanted, yes, no):
        test = jnp.full(no.shape, value, jnp.int32)
        return jnp.where(test == wanted, yes.astype(jnp.float32), no.astype(jnp.float32)).astype(BF16)

    moves = [start_ref[e] // tile_rows for e in range(members)]
    turns = [jnp.where(m > ring // 2, m - ring, m) for m in moves]
    high = [jnp.where(t >= 2, 1, jnp.where(t <= -2, -1, 0)) for t in turns]
    low = [t - 3 * h for t, h in zip(turns, high)]

    for e in range(1, members):
        for h in range(2):
            for i in range(2):
                turned(e, 0, i, h).start()

    window[0, tile_rows : 2 * tile_rows, :] = x_ref[0]
    @pl.when(last_first)
    def _():
        for h in range(2):
            over(0, h).start()

    ship(0, (1, 2))

    @pl.when(jnp.logical_not(last_second))
    def _():
        each(0, own(0), (0,), lambda n, i, src: parcel(0, n, i, src).start())

    @pl.when(first_second)
    def _():
        end(2).start()

    tap = lax.broadcasted_iota(jnp.int32, (side, LANES), 0)
    spot = lax.broadcasted_iota(jnp.int32, (side, LANES), 1)
    reverse = jnp.where((tap + spot == LANES) | (tap + spot == 0), 1.0, 0.0).astype(BF16)
    for k in range(kernels):
        seeds = jnp.dot(basis_ref[k], reverse, preferred_element_type=jnp.float32)
        for a in range(side):
            seed = jnp.broadcast_to(seeds[a : a + 1, :], (LANES, LANES))
            band = pltpu.roll(seed, 0, 1, stride=1, stride_axis=0)
            table[a * LANES : (a + 1) * LANES, k * LANES : (k + 1) * LANES] = band.astype(BF16)

    def turn_high(e, h):
        for i in range(2):
            turned(e, 0, i, h).wait_recv()
        at = rows_of(h)
        held[e, at] = choose(
            high[e], 1, far[e, 0, at], choose(high[e], -1, far[e, 1, at], x_ref[e, at])
        )
        for i in range(2):
            turned(e, 1, i, h).start()

    def turn_low(e, h):
        for i in range(2):
            turned(e, 1, i, h).wait_recv()
        at = rows_of(h)
        window[e, own_rows(h), :] = choose(
            low[e], 1, near[e, 0, at], choose(low[e], -1, near[e, 1, at], held[e, at])
        )

        @pl.when(second == 0)
        def _():
            over(e, h).start()
            if h == 1:
                ship(e, (0, 1, 2))

    halves = [(e, h) for e in range(1, members) for h in range(2)]
    lag = 3
    for j in range(len(halves) + lag):
        if j < len(halves):
            turn_high(*halves[j])
        if j >= lag:
            turn_low(*halves[j - lag])

    @pl.when(last_second)
    def _():
        for h in range(2):
            over(0, h).wait_recv()
        each(0, across.at[0], (0,), lambda n, i, src: parcel(0, n, i, src).start())

    all_rows, lead = shifted.shape[1], tile_rows - 2 * half
    window_rows = row_base - tile_rows + lax.broadcasted_iota(jnp.int32, (all_rows, LANES), 0)
    lane_in = lax.broadcasted_iota(jnp.int32, (all_rows, LANES), 1)
    out_row = row_base - half + lax.broadcasted_iota(jnp.int32, (rows, LANES), 0)
    y = (2 * out_row + 1).astype(jnp.float32) / band_rows - 1.0
    lane = lax.broadcasted_iota(jnp.int32, (rows, LANES), 1)
    cols = [col_base - half + block * step + lane for block in range(blocks)]

    def match(e):
        @pl.when(last_first)
        def _():
            after = slice(2 * tile_rows, 3 * tile_rows)
            window[e, after, :] = choose(moves[e], 0, cross[e], window[e, after, :])
            for i in range(2):
                edges[i, e, after, :] = choose(
                    moves[e], 0, cross_edges[i, e], edges[i, e, after, :]
                )

        first, total = start_ref[e], count_ref[e]
        inside = (out_row >= first) & (out_row < first + total)
        weighting = weight_ref[e] * inside.astype(jnp.float32)
        valid = (window_rows >= first) & (window_rows < first + total)
        pieces = [edges[0, e]]
        for tile in range(tile_cols // LANES):
            pieces.append(window[e, :, tile * LANES : (tile + 1) * LANES])
        pieces.append(edges[1, e])
        parts = []
        for tile, piece in enumerate(pieces):
            col = lane_in + (col_base + (tile - 1) * LANES)
            keep = valid & (col >= 0) & (col < band_cols)
            parts.append(jnp.where(keep, piece.astype(jnp.float32), 0.0))
        for block in range(blocks):
            tile, offset = divmod(LANES - 2 * half + block * step, LANES)
            here = parts[tile]
            if offset:
                here = pltpu.roll(here, LANES - offset, 1)
                after = pltpu.roll(parts[tile + 1], LANES - offset, 1)
                here = jnp.where(lane_in < LANES - offset, here, after)
            shifted[block] = here
        for a in range(side):
            piece = jnp.concatenate(
                [shifted[block, lead + a : lead + a + rows, :] for block in range(blocks)], axis=0
            )
            lhs[:, a * LANES : (a + 1) * LANES] = piece.astype(BF16)
        response = jnp.dot(lhs[...], table[...], preferred_element_type=jnp.float32)
        for block in range(blocks):
            x = (2 * cols[block] + 1).astype(jnp.float32) / band_cols - 1.0
            matched = jnp.zeros((rows, LANES), jnp.float32)
            for k in range(kernels):
                p = [poly_ref[k, e, i] for i in range(6)]
                spatial = (p[0] + y * (p[2] + p[5] * y)) + x * ((p[1] + p[4] * y) + p[3] * x)
                matched = matched + spatial * response[
                    block * rows : (block + 1) * rows, k * LANES : (k + 1) * LANES
                ]
            if e == 0:
                sums[block] = weighting * matched
            else:
                sums[block] += weighting * matched
    @pl.when(last_first)
    def _():
        end(2).wait_recv()

    for i in range(2):

        @pl.when(last_first & has[i])
        def _(i=i):
            end(i).start()

    for i in range(2):

        @pl.when(last_first & has[1 - i])
        def _(i=i):
            end(i).wait_recv()

    arrive(0)
    match(0)
    for e in range(1, members):

        @pl.when(second == 1)
        def _(e=e):
            for h in range(2):
                over(e, h).wait_recv()
            here = window[e, tile_rows : 2 * tile_rows, :].astype(jnp.float32)
            passed = jnp.full(here.shape, moves[e] - place, jnp.int32)
            chosen = jnp.where(passed > 0, across[e].astype(jnp.float32), here)
            window[e, tile_rows : 2 * tile_rows, :] = chosen.astype(BF16)
            ship(e, (0, 1, 2))

    denominator = jnp.zeros((rows, LANES), jnp.float32)
    for e in range(members):
        inside = (out_row >= start_ref[e]) & (out_row < start_ref[e] + count_ref[e])
        denominator = denominator + weight_ref[e] * inside.astype(jnp.float32)
    in_rows = (out_row >= 0) & (out_row < band_rows)
    inverse = 1.0 / jnp.where(in_rows, denominator, 1.0)

    for e in range(1, members):
        arrive(e)
        match(e)

    coadds = []
    for block in range(blocks):
        keep = in_rows & (cols[block] >= 0) & (cols[block] < band_cols)
        coadds.append(jnp.where(keep, sums[block] * inverse, 0.0))
    tiles = spread.shape[1] // LANES
    for tile in range(tiles):
        line = jnp.zeros((rows, LANES), jnp.float32)
        for block in range(blocks):
            low = block * step - tile * LANES
            if low + step <= 0 or low >= LANES:
                continue
            rolled = pltpu.roll(coadds[block], low % LANES, 1) if low % LANES else coadds[block]
            line = jnp.where((lane >= low) & (lane < low + step), rolled, line)
        spread[:, tile * LANES : (tile + 1) * LANES] = line

    def ahead(parts, tile, offset):
        if offset == 0:
            return parts[tile]
        lanes = lax.broadcasted_iota(jnp.int32, parts[tile].shape, 1)
        here = pltpu.roll(parts[tile], LANES - offset, 1)
        after = pltpu.roll(parts[tile + 1], LANES - offset, 1)
        return jnp.where(lanes < LANES - offset, here, after)

    out_tiles = tile_cols // LANES
    mine = [
        spread[half : half + tile_rows, i * LANES : (i + 1) * LANES] for i in range(tiles)
    ]
    for i in range(out_tiles):
        result_ref[0, :, i * LANES : (i + 1) * LANES] = ahead(mine, i, half)
    down = []
    for i in range(tiles):
        total = taps_ref[0] * spread[0:tile_rows, i * LANES : (i + 1) * LANES]
        for t in range(1, side):
            total = total + taps_ref[t] * spread[
                t : t + tile_rows, i * LANES : (i + 1) * LANES
            ]
        down.append(total)
    totals = [taps_ref[0] * down[i] for i in range(out_tiles)]
    lanes = lax.broadcasted_iota(jnp.int32, down[0].shape, 1)
    for t in range(1, side):
        rolled = [pltpu.roll(part, LANES - t, 1) for part in down]
        for i in range(out_tiles):
            here = jnp.where(lanes < LANES - t, rolled[i], rolled[i + 1])
            totals[i] = totals[i] + taps_ref[t] * here
    for i in range(out_tiles):
        result_ref[1, :, i * LANES : (i + 1) * LANES] = totals[i]

    for e in range(1, members):
        for stage in range(2):
            for i in range(2):
                for h in range(2):
                    turned(e, stage, i, h).wait_send()

    @pl.when(second == 0)
    def _():
        for e in range(1, members):
            for h in range(2):
                over(e, h).wait_send()

    @pl.when(last_first)
    def _():
        for h in range(2):
            over(0, h).wait_send()

    @pl.when(first_second)
    def _():
        end(2).wait_send()

    for i in range(2):

        @pl.when(last_first & has[i])
        def _(i=i):
            end(i).wait_send()

    for e in range(members):
        each(e, own(e), (0, 1, 2), lambda n, i, src, e=e: parcel(e, n, i, src).wait_send())


def on_device(
    exposures, basis_kernels, poly_coef, exposure_weight, row_start, row_count, filter_taps
):
    members, tile_rows, tile_cols = exposures.shape
    kernels, side = basis_kernels.shape[:2]
    half = side // 2
    band_rows = tile_rows * lax.axis_size("narrow")
    band_cols = tile_cols * lax.axis_size("wide")
    step = LANES - (side - 1)
    blocks = pl.cdiv(tile_cols + 2 * half, step)
    rows = pl.cdiv(tile_rows + 2 * half, SUBLANES) * SUBLANES
    all_rows = 3 * tile_rows
    width = pl.cdiv(tile_cols + 2 * half, LANES) * LANES
    sizes = (members, kernels, side, band_rows, band_cols, tile_rows, tile_cols)
    out = jax.ShapeDtypeStruct((2, tile_rows, tile_cols), jnp.float32)
    scalars = pl.BlockSpec(memory_space=pltpu.SMEM)
    vmem = pl.BlockSpec(memory_space=pltpu.VMEM)
    dma = pltpu.SemaphoreType.DMA
    results = pl.pallas_call(
        functools.partial(whole_kernel, sizes),
        out_shape=out,
        in_specs=[scalars] * 5 + [pl.BlockSpec(memory_space=pl.ANY), vmem],
        out_specs=vmem,
        scratch_shapes=[
            pltpu.VMEM((members, tile_rows, tile_cols), BF16),
            pltpu.VMEM((members, all_rows, tile_cols), BF16),
            pltpu.VMEM((2, members, all_rows, LANES), BF16),
            pltpu.VMEM((members, 2, tile_rows, tile_cols), BF16),
            pltpu.VMEM((members, 2, tile_rows, tile_cols), BF16),
            pltpu.VMEM((members, tile_rows, tile_cols), BF16),
            pltpu.VMEM((members, tile_rows, tile_cols), BF16),
            pltpu.VMEM((2, members, tile_rows, LANES), BF16),
            pltpu.VMEM((members, tile_rows, tile_cols), BF16),
            pltpu.VMEM((side * LANES, kernels * LANES), BF16),
            pltpu.VMEM((blocks, all_rows, LANES), jnp.float32),
            pltpu.VMEM((blocks * rows, side * LANES), BF16),
            pltpu.VMEM((blocks, rows, LANES), jnp.float32),
            pltpu.VMEM((rows, width), jnp.float32),
            dma((8 * members,)),
            dma((8 * members,)),
            dma((2 * members,)),
            dma((2 * members,)),
            dma((3,)),
            dma((3,)),
            dma((9 * members,)),
            dma((9 * members,)),
            dma,
        ],
        compiler_params=pltpu.CompilerParams(collective_id=0, has_side_effects=True),
        name="whole",
    )(poly_coef.transpose(1, 0, 2), exposure_weight, row_start, row_count, filter_taps, exposures, basis_kernels)
    return results[0], results[1]


def solution(mesh):
    placed = (P(None, "narrow", "wide"), P(), P(), P(), P(), P(), P())
    return jax.shard_map(
        on_device,
        mesh=mesh,
        in_specs=placed,
        out_specs=(P("narrow", "wide"), P("narrow", "wide")),
        check_vma=False,
    )
```

```python
import functools

import jax
import jax.numpy as jnp
from jax import lax
from jax.experimental import pallas as pl
from jax.experimental.pallas import tpu as pltpu
from jax.sharding import PartitionSpec as P

LANES = 128
SUBLANES = 8


MESH = pl.DeviceIdType.MESH
BF16 = jnp.bfloat16


def whole_kernel(
    sizes,
    poly_ref,
    weight_ref,
    start_ref,
    count_ref,
    taps_ref,
    x_hbm,
    basis_ref,
    result_ref,
    x_ref,
    window,
    edges,
    far,
    near,
    across,
    cross,
    cross_edges,
    held,
    table,
    shifted,
    lhs,
    sums,
    spread,
    turn_sent,
    turn_got,
    over_sent,
    over_got,
    end_sent,
    end_got,
    ship_sent,
    ship_got,
    fetched,
):
    members, kernels, side, band_rows, band_cols, tile_rows, tile_cols = sizes
    half = side // 2
    step = LANES - (side - 1)
    blocks = pl.cdiv(tile_cols + 2 * half, step)
    rows = pl.cdiv(tile_rows + 2 * half, SUBLANES) * SUBLANES
    ring = lax.axis_size("narrow") // 2
    me = lax.axis_index("narrow")
    column, columns = lax.axis_index("wide"), lax.axis_size("wide")
    second, place = me // ring, me % ring
    row_base, col_base = me * tile_rows, column * tile_cols
    has = (column > 0, column < columns - 1)

    def on_ring(turn):
        return second * ring + (place + turn + ring) % ring

    last_first = (second == 0) & (place == ring - 1)
    first_second = (second == 1) & (place == 0)
    last_second = (second == 1) & (place == ring - 1)
    other = (1 - second) * ring + place
    over_end = (1 - second) * ring + (ring - 1 - place)

    fetch = pltpu.make_async_copy(x_hbm, x_ref, fetched)
    fetch.start()
    barrier = pltpu.get_barrier_semaphore()

    def greet(peer):
        pl.semaphore_signal(barrier, inc=1, device_id=peer, device_id_type=MESH)

    for peer in (on_ring(3), on_ring(-3), other):
        greet({"narrow": peer})
    for turn in (1, -1):
        greet({"narrow": on_ring(turn)})
    at_end = last_first | first_second
    count = 5 + at_end.astype(jnp.int32)

    @pl.when(at_end)
    def _():
        greet({"narrow": over_end})

    for i in range(2):
        beside = column + 2 * i - 1

        @pl.when(has[i])
        def _(beside=beside):
            greet({"wide": beside})
            for turn in (1, -1):
                greet({"narrow": on_ring(turn), "wide": beside})

        count = count + 3 * has[i].astype(jnp.int32)

    fetch.wait()
    pl.semaphore_wait(barrier, count)

    def copy(src, dst, send_sem, recv_sem, peer):
        return pltpu.make_async_remote_copy(
            src_ref=src,
            dst_ref=dst,
            send_sem=send_sem,
            recv_sem=recv_sem,
            device_id=peer,
            device_id_type=MESH,
        )

    def own(e):
        return window.at[e, tile_rows : 2 * tile_rows, :]

    def turned(e, stage, i):
        src, into, by = ((x_ref, far, 3), (held, near, 1))[stage]
        slot = (2 * e + stage) * 2 + i
        peer = {"narrow": on_ring(by - 2 * by * i)}
        return copy(src.at[e], into.at[e, i], turn_sent.at[slot], turn_got.at[slot], peer)

    def over(e):
        return copy(own(e), across.at[e], over_sent.at[e], over_got.at[e], {"narrow": other})

    def lanes_of(i):
        return slice(0, LANES) if i == 0 else slice(tile_cols - LANES, tile_cols)

    def end(i):
        if i == 2:
            return copy(x_ref, cross, end_sent.at[2], end_got.at[2], {"narrow": over_end})
        return copy(
            cross.at[:, :, lanes_of(i)],
            cross_edges.at[1 - i],
            end_sent.at[i],
            end_got.at[i],
            {"wide": column + 2 * i - 1},
        )

    def parcel(e, n, i, src):
        slot = (3 * e + n) * 3 + i
        where = slice(n * tile_rows, (n + 1) * tile_rows)
        peer = {"narrow": on_ring(1 - n)} if n != 1 else {}
        if i == 2:
            dst = window.at[e, where, :]
        else:
            peer["wide"] = column + 2 * i - 1
            src, dst = src.at[:, lanes_of(i)], edges.at[1 - i, e, where, :]
        return copy(src, dst, ship_sent.at[slot], ship_got.at[slot], peer)

    def each(e, src, steps, act):
        for n in steps:
            for i in (2, 0, 1):
                if i == 2:
                    if n != 1:
                        act(n, i, src)
                else:

                    @pl.when(has[i])
                    def _(n=n, i=i):
                        act(n, i, src)

    def ship(e, steps):
        if 0 in steps:

            @pl.when(last_second)
            def _():
                each(e, across.at[e], (0,), lambda n, i, src: parcel(e, n, i, src).start())

            @pl.when(jnp.logical_not(last_second))
            def _():
                each(e, own(e), (0,), lambda n, i, src: parcel(e, n, i, src).start())

        rest = tuple(n for n in steps if n)
        each(e, own(e), rest, lambda n, i, src: parcel(e, n, i, src).start())

    def arrive(e):
        for n in (0, 2):
            parcel(e, n, 2, own(e)).wait_recv()
        for i in range(2):

            @pl.when(has[1 - i])
            def _(i=i):
                for n in range(3):
                    parcel(e, n, i, own(e)).wait_recv()

    def choose(value, wanted, yes, no):
        test = jnp.full(no.shape, value, jnp.int32)
        return jnp.where(test == wanted, yes.astype(jnp.float32), no.astype(jnp.float32)).astype(BF16)

    moves = [start_ref[e] // tile_rows for e in range(members)]
    turns = [jnp.where(m > ring // 2, m - ring, m) for m in moves]
    high = [jnp.where(t >= 2, 1, jnp.where(t <= -2, -1, 0)) for t in turns]
    low = [t - 3 * h for t, h in zip(turns, high)]

    for e in range(1, members):
        for i in range(2):
            turned(e, 0, i).start()

    window[0, tile_rows : 2 * tile_rows, :] = x_ref[0]
    @pl.when(last_first)
    def _():
        over(0).start()

    ship(0, (1, 2))

    @pl.when(jnp.logical_not(last_second))
    def _():
        each(0, own(0), (0,), lambda n, i, src: parcel(0, n, i, src).start())

    @pl.when(first_second)
    def _():
        end(2).start()

    tap = lax.broadcasted_iota(jnp.int32, (side, LANES), 0)
    spot = lax.broadcasted_iota(jnp.int32, (side, LANES), 1)
    reverse = jnp.where((tap + spot == LANES) | (tap + spot == 0), 1.0, 0.0).astype(BF16)
    for k in range(kernels):
        seeds = jnp.dot(basis_ref[k], reverse, preferred_element_type=jnp.float32)
        for a in range(side):
            seed = jnp.broadcast_to(seeds[a : a + 1, :], (LANES, LANES))
            band = pltpu.roll(seed, 0, 1, stride=1, stride_axis=0)
            table[a * LANES : (a + 1) * LANES, k * LANES : (k + 1) * LANES] = band.astype(BF16)

    for e in range(1, members):
        for i in range(2):
            turned(e, 0, i).wait_recv()
        held[e] = choose(high[e], 1, far[e, 0], choose(high[e], -1, far[e, 1], x_ref[e]))
        for i in range(2):
            turned(e, 1, i).start()

    @pl.when(last_second)
    def _():
        over(0).wait_recv()
        each(0, across.at[0], (0,), lambda n, i, src: parcel(0, n, i, src).start())

    for e in range(1, members):
        for i in range(2):
            turned(e, 1, i).wait_recv()
        window[e, tile_rows : 2 * tile_rows, :] = choose(
            low[e], 1, near[e, 0], choose(low[e], -1, near[e, 1], held[e])
        )

        @pl.when(second == 0)
        def _(e=e):
            over(e).start()
            ship(e, (0, 1, 2))

    all_rows, lead = shifted.shape[1], tile_rows - 2 * half
    window_rows = row_base - tile_rows + lax.broadcasted_iota(jnp.int32, (all_rows, LANES), 0)
    lane_in = lax.broadcasted_iota(jnp.int32, (all_rows, LANES), 1)
    out_row = row_base - half + lax.broadcasted_iota(jnp.int32, (rows, LANES), 0)
    y = (2 * out_row + 1).astype(jnp.float32) / band_rows - 1.0
    lane = lax.broadcasted_iota(jnp.int32, (rows, LANES), 1)
    cols = [col_base - half + block * step + lane for block in range(blocks)]

    def match(e):
        @pl.when(last_first)
        def _():
            after = slice(2 * tile_rows, 3 * tile_rows)
            window[e, after, :] = choose(moves[e], 0, cross[e], window[e, after, :])
            for i in range(2):
                edges[i, e, after, :] = choose(
                    moves[e], 0, cross_edges[i, e], edges[i, e, after, :]
                )

        first, total = start_ref[e], count_ref[e]
        inside = (out_row >= first) & (out_row < first + total)
        weighting = weight_ref[e] * inside.astype(jnp.float32)
        valid = (window_rows >= first) & (window_rows < first + total)
        pieces = [edges[0, e]]
        for tile in range(tile_cols // LANES):
            pieces.append(window[e, :, tile * LANES : (tile + 1) * LANES])
        pieces.append(edges[1, e])
        parts = []
        for tile, piece in enumerate(pieces):
            col = lane_in + (col_base + (tile - 1) * LANES)
            keep = valid & (col >= 0) & (col < band_cols)
            parts.append(jnp.where(keep, piece.astype(jnp.float32), 0.0))
        for block in range(blocks):
            tile, offset = divmod(LANES - 2 * half + block * step, LANES)
            here = parts[tile]
            if offset:
                here = pltpu.roll(here, LANES - offset, 1)
                after = pltpu.roll(parts[tile + 1], LANES - offset, 1)
                here = jnp.where(lane_in < LANES - offset, here, after)
            shifted[block] = here
        for a in range(side):
            piece = jnp.concatenate(
                [shifted[block, lead + a : lead + a + rows, :] for block in range(blocks)], axis=0
            )
            lhs[:, a * LANES : (a + 1) * LANES] = piece.astype(BF16)
        response = jnp.dot(lhs[...], table[...], preferred_element_type=jnp.float32)
        for block in range(blocks):
            x = (2 * cols[block] + 1).astype(jnp.float32) / band_cols - 1.0
            matched = jnp.zeros((rows, LANES), jnp.float32)
            for k in range(kernels):
                p = [poly_ref[k, e, i] for i in range(6)]
                spatial = (p[0] + y * (p[2] + p[5] * y)) + x * ((p[1] + p[4] * y) + p[3] * x)
                matched = matched + spatial * response[
                    block * rows : (block + 1) * rows, k * LANES : (k + 1) * LANES
                ]
            if e == 0:
                sums[block] = weighting * matched
            else:
                sums[block] += weighting * matched
    @pl.when(last_first)
    def _():
        end(2).wait_recv()

    for i in range(2):

        @pl.when(last_first & has[i])
        def _(i=i):
            end(i).start()

    for i in range(2):

        @pl.when(last_first & has[1 - i])
        def _(i=i):
            end(i).wait_recv()

    arrive(0)
    match(0)
    for e in range(1, members):

        @pl.when(second == 1)
        def _(e=e):
            over(e).wait_recv()
            here = window[e, tile_rows : 2 * tile_rows, :].astype(jnp.float32)
            passed = jnp.full(here.shape, moves[e] - place, jnp.int32)
            chosen = jnp.where(passed > 0, across[e].astype(jnp.float32), here)
            window[e, tile_rows : 2 * tile_rows, :] = chosen.astype(BF16)
            ship(e, (0, 1, 2))

    denominator = jnp.zeros((rows, LANES), jnp.float32)
    for e in range(members):
        inside = (out_row >= start_ref[e]) & (out_row < start_ref[e] + count_ref[e])
        denominator = denominator + weight_ref[e] * inside.astype(jnp.float32)
    in_rows = (out_row >= 0) & (out_row < band_rows)
    inverse = 1.0 / jnp.where(in_rows, denominator, 1.0)

    for e in range(1, members):
        arrive(e)
        match(e)

    coadds = []
    for block in range(blocks):
        keep = in_rows & (cols[block] >= 0) & (cols[block] < band_cols)
        coadds.append(jnp.where(keep, sums[block] * inverse, 0.0))
    tiles = spread.shape[1] // LANES
    for tile in range(tiles):
        line = jnp.zeros((rows, LANES), jnp.float32)
        for block in range(blocks):
            low = block * step - tile * LANES
            if low + step <= 0 or low >= LANES:
                continue
            rolled = pltpu.roll(coadds[block], low % LANES, 1) if low % LANES else coadds[block]
            line = jnp.where((lane >= low) & (lane < low + step), rolled, line)
        spread[:, tile * LANES : (tile + 1) * LANES] = line

    for i in range(tiles):
        at = slice(i * LANES, (i + 1) * LANES)
        result_ref[0, :, at] = spread[half : half + tile_rows, at]
        total = taps_ref[0] * spread[0:tile_rows, at]
        for t in range(1, side):
            total = total + taps_ref[t] * spread[t : t + tile_rows, at]
        result_ref[1, :, at] = total

    for e in range(1, members):
        for stage in range(2):
            for i in range(2):
                turned(e, stage, i).wait_send()

    @pl.when(second == 0)
    def _():
        for e in range(1, members):
            over(e).wait_send()

    @pl.when(last_first)
    def _():
        over(0).wait_send()

    @pl.when(first_second)
    def _():
        end(2).wait_send()

    for i in range(2):

        @pl.when(last_first & has[i])
        def _(i=i):
            end(i).wait_send()

    for e in range(members):
        each(e, own(e), (0, 1, 2), lambda n, i, src, e=e: parcel(e, n, i, src).wait_send())


def across_kernel(side, taps_ref, rows_ref, coadd_ref, detect_ref):
    half = side // 2
    tiles = rows_ref.shape[2] // LANES
    own, down = [
        [rows_ref[n, :, i * LANES : (i + 1) * LANES] for i in range(tiles)] for n in range(2)
    ]
    lanes = lax.broadcasted_iota(jnp.int32, down[0].shape, 1)

    def ahead(parts, t):
        rolled = [pltpu.roll(part, LANES - t, 1) for part in parts]
        return [jnp.where(lanes < LANES - t, a, b) for a, b in zip(rolled, rolled[1:])]

    for i, value in enumerate(ahead(own, half)):
        coadd_ref[:, i * LANES : (i + 1) * LANES] = value
    totals = [taps_ref[0] * part for part in down[:-1]]
    for t in range(1, side):
        totals = [total + taps_ref[t] * value for total, value in zip(totals, ahead(down, t))]
    for i, total in enumerate(totals):
        detect_ref[:, i * LANES : (i + 1) * LANES] = total


def on_device(
    exposures, basis_kernels, poly_coef, exposure_weight, row_start, row_count, filter_taps
):
    members, tile_rows, tile_cols = exposures.shape
    kernels, side = basis_kernels.shape[:2]
    half = side // 2
    band_rows = tile_rows * lax.axis_size("narrow")
    band_cols = tile_cols * lax.axis_size("wide")
    step = LANES - (side - 1)
    blocks = pl.cdiv(tile_cols + 2 * half, step)
    rows = pl.cdiv(tile_rows + 2 * half, SUBLANES) * SUBLANES
    all_rows = 3 * tile_rows
    width = pl.cdiv(tile_cols + 2 * half, LANES) * LANES
    sizes = (members, kernels, side, band_rows, band_cols, tile_rows, tile_cols)
    out = jax.ShapeDtypeStruct((tile_rows, tile_cols), jnp.float32)
    scalars = pl.BlockSpec(memory_space=pltpu.SMEM)
    vmem = pl.BlockSpec(memory_space=pltpu.VMEM)
    dma = pltpu.SemaphoreType.DMA
    results = pl.pallas_call(
        functools.partial(whole_kernel, sizes),
        out_shape=jax.ShapeDtypeStruct((2, tile_rows, width), jnp.float32),
        in_specs=[scalars] * 5 + [pl.BlockSpec(memory_space=pl.ANY), vmem],
        out_specs=vmem,
        scratch_shapes=[
            pltpu.VMEM((members, tile_rows, tile_cols), BF16),
            pltpu.VMEM((members, all_rows, tile_cols), BF16),
            pltpu.VMEM((2, members, all_rows, LANES), BF16),
            pltpu.VMEM((members, 2, tile_rows, tile_cols), BF16),
            pltpu.VMEM((members, 2, tile_rows, tile_cols), BF16),
            pltpu.VMEM((members, tile_rows, tile_cols), BF16),
            pltpu.VMEM((members, tile_rows, tile_cols), BF16),
            pltpu.VMEM((2, members, tile_rows, LANES), BF16),
            pltpu.VMEM((members, tile_rows, tile_cols), BF16),
            pltpu.VMEM((side * LANES, kernels * LANES), BF16),
            pltpu.VMEM((blocks, all_rows, LANES), jnp.float32),
            pltpu.VMEM((blocks * rows, side * LANES), BF16),
            pltpu.VMEM((blocks, rows, LANES), jnp.float32),
            pltpu.VMEM((rows, width), jnp.float32),
            dma((4 * members,)),
            dma((4 * members,)),
            dma((members,)),
            dma((members,)),
            dma((3,)),
            dma((3,)),
            dma((9 * members,)),
            dma((9 * members,)),
            dma,
        ],
        compiler_params=pltpu.CompilerParams(collective_id=0, has_side_effects=True),
        name="whole",
    )(poly_coef.transpose(1, 0, 2), exposure_weight, row_start, row_count, filter_taps, exposures, basis_kernels)
    return pl.pallas_call(
        functools.partial(across_kernel, side),
        out_shape=(out, out),
        in_specs=[scalars, vmem],
        out_specs=(vmem,) * 2,
        name="across",
    )(filter_taps, results)


def solution(mesh):
    placed = (P(None, "narrow", "wide"), P(), P(), P(), P(), P(), P())
    return jax.shard_map(
        on_device,
        mesh=mesh,
        in_specs=placed,
        out_specs=(P("narrow", "wide"), P("narrow", "wide")),
        check_vma=False,
    )
```

```python
import functools

import jax
import jax.numpy as jnp
from jax import lax
from jax.experimental import pallas as pl
from jax.experimental.pallas import tpu as pltpu
from jax.sharding import PartitionSpec as P

LANES = 128
SUBLANES = 8


MESH = pl.DeviceIdType.MESH
BF16 = jnp.bfloat16


def whole_kernel(
    sizes,
    poly_ref,
    weight_ref,
    start_ref,
    count_ref,
    taps_ref,
    x_hbm,
    basis_ref,
    result_ref,
    x_ref,
    window,
    edges,
    far,
    near,
    across,
    cross,
    cross_edges,
    held,
    table,
    shifted,
    lhs,
    sums,
    spread,
    turn_sent,
    turn_got,
    over_sent,
    over_got,
    end_sent,
    end_got,
    ship_sent,
    ship_got,
    fetched,
):
    members, kernels, side, band_rows, band_cols, tile_rows, tile_cols = sizes
    half = side // 2
    step = LANES - (side - 1)
    blocks = pl.cdiv(tile_cols + 2 * half, step)
    rows = pl.cdiv(tile_rows + 2 * half, SUBLANES) * SUBLANES
    ring = lax.axis_size("narrow") // 2
    me = lax.axis_index("narrow")
    column, columns = lax.axis_index("wide"), lax.axis_size("wide")
    second, place = me // ring, me % ring
    row_base, col_base = me * tile_rows, column * tile_cols
    has = (column > 0, column < columns - 1)

    def on_ring(turn):
        return second * ring + (place + turn + ring) % ring

    last_first = (second == 0) & (place == ring - 1)
    first_second = (second == 1) & (place == 0)
    last_second = (second == 1) & (place == ring - 1)
    other = (1 - second) * ring + place
    over_end = (1 - second) * ring + (ring - 1 - place)

    fetch = pltpu.make_async_copy(x_hbm, x_ref, fetched)
    fetch.start()
    barrier = pltpu.get_barrier_semaphore()

    def greet(peer):
        pl.semaphore_signal(barrier, inc=1, device_id=peer, device_id_type=MESH)

    for peer in (on_ring(3), on_ring(-3), other):
        greet({"narrow": peer})
    for turn in (1, -1):
        greet({"narrow": on_ring(turn)})
    at_end = last_first | first_second
    count = 5 + at_end.astype(jnp.int32)

    @pl.when(at_end)
    def _():
        greet({"narrow": over_end})

    for i in range(2):
        beside = column + 2 * i - 1

        @pl.when(has[i])
        def _(beside=beside):
            greet({"wide": beside})
            for turn in (1, -1):
                greet({"narrow": on_ring(turn), "wide": beside})

        count = count + 3 * has[i].astype(jnp.int32)

    fetch.wait()
    pl.semaphore_wait(barrier, count)

    def copy(src, dst, send_sem, recv_sem, peer):
        return pltpu.make_async_remote_copy(
            src_ref=src,
            dst_ref=dst,
            send_sem=send_sem,
            recv_sem=recv_sem,
            device_id=peer,
            device_id_type=MESH,
        )

    def own(e):
        return window.at[e, tile_rows : 2 * tile_rows, :]

    def turned(e, stage, i):
        src, into, by = ((x_ref, far, 3), (held, near, 1))[stage]
        slot = (2 * e + stage) * 2 + i
        peer = {"narrow": on_ring(by - 2 * by * i)}
        return copy(src.at[e], into.at[e, i], turn_sent.at[slot], turn_got.at[slot], peer)

    def over(e):
        return copy(own(e), across.at[e], over_sent.at[e], over_got.at[e], {"narrow": other})

    def lanes_of(i):
        return slice(0, LANES) if i == 0 else slice(tile_cols - LANES, tile_cols)

    def end(i):
        if i == 2:
            return copy(x_ref, cross, end_sent.at[2], end_got.at[2], {"narrow": over_end})
        return copy(
            cross.at[:, :, lanes_of(i)],
            cross_edges.at[1 - i],
            end_sent.at[i],
            end_got.at[i],
            {"wide": column + 2 * i - 1},
        )

    def parcel(e, n, i, src):
        slot = (3 * e + n) * 3 + i
        where = slice(n * tile_rows, (n + 1) * tile_rows)
        peer = {"narrow": on_ring(1 - n)} if n != 1 else {}
        if i == 2:
            dst = window.at[e, where, :]
        else:
            peer["wide"] = column + 2 * i - 1
            src, dst = src.at[:, lanes_of(i)], edges.at[1 - i, e, where, :]
        return copy(src, dst, ship_sent.at[slot], ship_got.at[slot], peer)

    def each(e, src, steps, act):
        for n in steps:
            for i in (2, 0, 1):
                if i == 2:
                    if n != 1:
                        act(n, i, src)
                else:

                    @pl.when(has[i])
                    def _(n=n, i=i):
                        act(n, i, src)

    def ship(e, steps):
        if 0 in steps:

            @pl.when(last_second)
            def _():
                each(e, across.at[e], (0,), lambda n, i, src: parcel(e, n, i, src).start())

            @pl.when(jnp.logical_not(last_second))
            def _():
                each(e, own(e), (0,), lambda n, i, src: parcel(e, n, i, src).start())

        rest = tuple(n for n in steps if n)
        each(e, own(e), rest, lambda n, i, src: parcel(e, n, i, src).start())

    def arrive(e):
        for n in (0, 2):
            parcel(e, n, 2, own(e)).wait_recv()
        for i in range(2):

            @pl.when(has[1 - i])
            def _(i=i):
                for n in range(3):
                    parcel(e, n, i, own(e)).wait_recv()

    def choose(value, wanted, yes, no):
        test = jnp.full(no.shape, value, jnp.int32)
        return jnp.where(test == wanted, yes.astype(jnp.float32), no.astype(jnp.float32)).astype(BF16)

    moves = [start_ref[e] // tile_rows for e in range(members)]
    turns = [jnp.where(m > ring // 2, m - ring, m) for m in moves]
    high = [jnp.where(t >= 2, 1, jnp.where(t <= -2, -1, 0)) for t in turns]
    low = [t - 3 * h for t, h in zip(turns, high)]

    for e in range(1, members):
        for i in range(2):
            turned(e, 0, i).start()

    window[0, tile_rows : 2 * tile_rows, :] = x_ref[0]
    @pl.when(last_first)
    def _():
        over(0).start()

    ship(0, (1, 2))

    @pl.when(jnp.logical_not(last_second))
    def _():
        each(0, own(0), (0,), lambda n, i, src: parcel(0, n, i, src).start())

    @pl.when(first_second)
    def _():
        end(2).start()

    tap = lax.broadcasted_iota(jnp.int32, (side, LANES), 0)
    spot = lax.broadcasted_iota(jnp.int32, (side, LANES), 1)
    reverse = jnp.where((tap + spot == LANES) | (tap + spot == 0), 1.0, 0.0).astype(BF16)
    for k in range(kernels):
        seeds = jnp.dot(basis_ref[k], reverse, preferred_element_type=jnp.float32)
        for a in range(side):
            seed = jnp.broadcast_to(seeds[a : a + 1, :], (LANES, LANES))
            band = pltpu.roll(seed, 0, 1, stride=1, stride_axis=0)
            table[a * LANES : (a + 1) * LANES, k * LANES : (k + 1) * LANES] = band.astype(BF16)

    for e in range(1, members):
        for i in range(2):
            turned(e, 0, i).wait_recv()
        held[e] = choose(high[e], 1, far[e, 0], choose(high[e], -1, far[e, 1], x_ref[e]))
        for i in range(2):
            turned(e, 1, i).start()

    @pl.when(last_second)
    def _():
        over(0).wait_recv()
        each(0, across.at[0], (0,), lambda n, i, src: parcel(0, n, i, src).start())

    for e in range(1, members):
        for i in range(2):
            turned(e, 1, i).wait_recv()
        window[e, tile_rows : 2 * tile_rows, :] = choose(
            low[e], 1, near[e, 0], choose(low[e], -1, near[e, 1], held[e])
        )

        @pl.when(second == 0)
        def _(e=e):
            over(e).start()
            ship(e, (0, 1, 2))

    all_rows, lead = shifted.shape[1], tile_rows - 2 * half
    window_rows = row_base - tile_rows + lax.broadcasted_iota(jnp.int32, (all_rows, LANES), 0)
    lane_in = lax.broadcasted_iota(jnp.int32, (all_rows, LANES), 1)
    out_row = row_base - half + lax.broadcasted_iota(jnp.int32, (rows, LANES), 0)
    y = (2 * out_row + 1).astype(jnp.float32) / band_rows - 1.0
    lane = lax.broadcasted_iota(jnp.int32, (rows, LANES), 1)
    cols = [col_base - half + block * step + lane for block in range(blocks)]

    def match(e):
        @pl.when(last_first)
        def _():
            after = slice(2 * tile_rows, 3 * tile_rows)
            window[e, after, :] = choose(moves[e], 0, cross[e], window[e, after, :])
            for i in range(2):
                edges[i, e, after, :] = choose(
                    moves[e], 0, cross_edges[i, e], edges[i, e, after, :]
                )

        first, total = start_ref[e], count_ref[e]
        inside = (out_row >= first) & (out_row < first + total)
        weighting = weight_ref[e] * inside.astype(jnp.float32)
        valid = (window_rows >= first) & (window_rows < first + total)
        pieces = [edges[0, e]]
        for tile in range(tile_cols // LANES):
            pieces.append(window[e, :, tile * LANES : (tile + 1) * LANES])
        pieces.append(edges[1, e])
        parts = []
        for tile, piece in enumerate(pieces):
            col = lane_in + (col_base + (tile - 1) * LANES)
            keep = valid & (col >= 0) & (col < band_cols)
            parts.append(jnp.where(keep, piece.astype(jnp.float32), 0.0))
        for block in range(blocks):
            tile, offset = divmod(LANES - 2 * half + block * step, LANES)
            here = parts[tile]
            if offset:
                here = pltpu.roll(here, LANES - offset, 1)
                after = pltpu.roll(parts[tile + 1], LANES - offset, 1)
                here = jnp.where(lane_in < LANES - offset, here, after)
            shifted[block] = here
        for a in range(side):
            piece = jnp.concatenate(
                [shifted[block, lead + a : lead + a + rows, :] for block in range(blocks)], axis=0
            )
            lhs[:, a * LANES : (a + 1) * LANES] = piece.astype(BF16)
        response = jnp.dot(lhs[...], table[...], preferred_element_type=jnp.float32)
        for block in range(blocks):
            x = (2 * cols[block] + 1).astype(jnp.float32) / band_cols - 1.0
            matched = jnp.zeros((rows, LANES), jnp.float32)
            for k in range(kernels):
                p = [poly_ref[k, e, i] for i in range(6)]
                spatial = (p[0] + y * (p[2] + p[5] * y)) + x * ((p[1] + p[4] * y) + p[3] * x)
                matched = matched + spatial * response[
                    block * rows : (block + 1) * rows, k * LANES : (k + 1) * LANES
                ]
            if e == 0:
                sums[block] = weighting * matched
            else:
                sums[block] += weighting * matched
    for e in range(1, members):

        @pl.when(second == 1)
        def _(e=e):
            over(e).wait_recv()
            here = window[e, tile_rows : 2 * tile_rows, :].astype(jnp.float32)
            passed = jnp.full(here.shape, moves[e] - place, jnp.int32)
            chosen = jnp.where(passed > 0, across[e].astype(jnp.float32), here)
            window[e, tile_rows : 2 * tile_rows, :] = chosen.astype(BF16)
            ship(e, (0, 1, 2))

    @pl.when(last_first)
    def _():
        end(2).wait_recv()

    for i in range(2):

        @pl.when(last_first & has[i])
        def _(i=i):
            end(i).start()

    for i in range(2):

        @pl.when(last_first & has[1 - i])
        def _(i=i):
            end(i).wait_recv()

    arrive(0)
    match(0)
    denominator = jnp.zeros((rows, LANES), jnp.float32)
    for e in range(members):
        inside = (out_row >= start_ref[e]) & (out_row < start_ref[e] + count_ref[e])
        denominator = denominator + weight_ref[e] * inside.astype(jnp.float32)
    in_rows = (out_row >= 0) & (out_row < band_rows)
    inverse = 1.0 / jnp.where(in_rows, denominator, 1.0)

    for e in range(1, members):
        arrive(e)
        match(e)

    coadds = []
    for block in range(blocks):
        keep = in_rows & (cols[block] >= 0) & (cols[block] < band_cols)
        coadds.append(jnp.where(keep, sums[block] * inverse, 0.0))
    tiles = spread.shape[1] // LANES
    for tile in range(tiles):
        line = jnp.zeros((rows, LANES), jnp.float32)
        for block in range(blocks):
            low = block * step - tile * LANES
            if low + step <= 0 or low >= LANES:
                continue
            rolled = pltpu.roll(coadds[block], low % LANES, 1) if low % LANES else coadds[block]
            line = jnp.where((lane >= low) & (lane < low + step), rolled, line)
        spread[:, tile * LANES : (tile + 1) * LANES] = line

    def ahead(parts, tile, offset):
        if offset == 0:
            return parts[tile]
        lanes = lax.broadcasted_iota(jnp.int32, parts[tile].shape, 1)
        here = pltpu.roll(parts[tile], LANES - offset, 1)
        after = pltpu.roll(parts[tile + 1], LANES - offset, 1)
        return jnp.where(lanes < LANES - offset, here, after)

    out_tiles = tile_cols // LANES
    mine = [
        spread[half : half + tile_rows, i * LANES : (i + 1) * LANES] for i in range(tiles)
    ]
    for i in range(out_tiles):
        result_ref[0, :, i * LANES : (i + 1) * LANES] = ahead(mine, i, half)
    down = []
    for i in range(tiles):
        total = taps_ref[0] * spread[0:tile_rows, i * LANES : (i + 1) * LANES]
        for t in range(1, side):
            total = total + taps_ref[t] * spread[
                t : t + tile_rows, i * LANES : (i + 1) * LANES
            ]
        down.append(total)
    totals = [taps_ref[0] * down[i] for i in range(out_tiles)]
    lanes = lax.broadcasted_iota(jnp.int32, down[0].shape, 1)
    for t in range(1, side):
        rolled = [pltpu.roll(part, LANES - t, 1) for part in down]
        for i in range(out_tiles):
            here = jnp.where(lanes < LANES - t, rolled[i], rolled[i + 1])
            totals[i] = totals[i] + taps_ref[t] * here
    for i in range(out_tiles):
        result_ref[1, :, i * LANES : (i + 1) * LANES] = totals[i]

    for e in range(1, members):
        for stage in range(2):
            for i in range(2):
                turned(e, stage, i).wait_send()

    @pl.when(second == 0)
    def _():
        for e in range(1, members):
            over(e).wait_send()

    @pl.when(last_first)
    def _():
        over(0).wait_send()

    @pl.when(first_second)
    def _():
        end(2).wait_send()

    for i in range(2):

        @pl.when(last_first & has[i])
        def _(i=i):
            end(i).wait_send()

    for e in range(members):
        each(e, own(e), (0, 1, 2), lambda n, i, src, e=e: parcel(e, n, i, src).wait_send())


def on_device(
    exposures, basis_kernels, poly_coef, exposure_weight, row_start, row_count, filter_taps
):
    members, tile_rows, tile_cols = exposures.shape
    kernels, side = basis_kernels.shape[:2]
    half = side // 2
    band_rows = tile_rows * lax.axis_size("narrow")
    band_cols = tile_cols * lax.axis_size("wide")
    step = LANES - (side - 1)
    blocks = pl.cdiv(tile_cols + 2 * half, step)
    rows = pl.cdiv(tile_rows + 2 * half, SUBLANES) * SUBLANES
    all_rows = 3 * tile_rows
    width = pl.cdiv(tile_cols + 2 * half, LANES) * LANES
    sizes = (members, kernels, side, band_rows, band_cols, tile_rows, tile_cols)
    out = jax.ShapeDtypeStruct((2, tile_rows, tile_cols), jnp.float32)
    scalars = pl.BlockSpec(memory_space=pltpu.SMEM)
    vmem = pl.BlockSpec(memory_space=pltpu.VMEM)
    dma = pltpu.SemaphoreType.DMA
    results = pl.pallas_call(
        functools.partial(whole_kernel, sizes),
        out_shape=out,
        in_specs=[scalars] * 5 + [pl.BlockSpec(memory_space=pl.ANY), vmem],
        out_specs=vmem,
        scratch_shapes=[
            pltpu.VMEM((members, tile_rows, tile_cols), BF16),
            pltpu.VMEM((members, all_rows, tile_cols), BF16),
            pltpu.VMEM((2, members, all_rows, LANES), BF16),
            pltpu.VMEM((members, 2, tile_rows, tile_cols), BF16),
            pltpu.VMEM((members, 2, tile_rows, tile_cols), BF16),
            pltpu.VMEM((members, tile_rows, tile_cols), BF16),
            pltpu.VMEM((members, tile_rows, tile_cols), BF16),
            pltpu.VMEM((2, members, tile_rows, LANES), BF16),
            pltpu.VMEM((members, tile_rows, tile_cols), BF16),
            pltpu.VMEM((side * LANES, kernels * LANES), BF16),
            pltpu.VMEM((blocks, all_rows, LANES), jnp.float32),
            pltpu.VMEM((blocks * rows, side * LANES), BF16),
            pltpu.VMEM((blocks, rows, LANES), jnp.float32),
            pltpu.VMEM((rows, width), jnp.float32),
            dma((4 * members,)),
            dma((4 * members,)),
            dma((members,)),
            dma((members,)),
            dma((3,)),
            dma((3,)),
            dma((9 * members,)),
            dma((9 * members,)),
            dma,
        ],
        compiler_params=pltpu.CompilerParams(collective_id=0, has_side_effects=True),
        name="whole",
    )(poly_coef.transpose(1, 0, 2), exposure_weight, row_start, row_count, filter_taps, exposures, basis_kernels)
    return results[0], results[1]


def solution(mesh):
    placed = (P(None, "narrow", "wide"), P(), P(), P(), P(), P(), P())
    return jax.shard_map(
        on_device,
        mesh=mesh,
        in_specs=placed,
        out_specs=(P("narrow", "wide"), P("narrow", "wide")),
        check_vma=False,
    )
```
